512 devices in a mesh: dp: 2 (over core), tensor: 4 (over x), expert: 64 (over y, z).
Axes of the slice: x: 4, y: 8, z: 8, core: 2. Of those that a mesh axis runs over, the one named last changes fastest.
Arguments:
- checkpoint: bfloat16 [16384, 2048], P(('dp', 'expert'), 'tensor'), may hold values from -6 to 6
- scales: float32 [16384], P(('dp', 'expert')), may hold values from 0.5 to 2
- out_grad: bfloat16 [16384, 2048], P(('dp', 'expert'), 'tensor'), may hold values from -1.5 to 1.5
- expert_ids: int32 [16384, 8], P(('dp', 'expert')), may hold values from 0 to 127, all different within a row; in each aligned block of 128 rows (0 to 127, 128 to 255, ...) at most 8 rows name the same one
- gates: float32 [16384, 8], P(('dp', 'expert')), may hold values from 0.05 to 1
- w_gate: bfloat16 [128, 768, 2048], P(('dp', 'expert'), 'tensor'), may hold values from -0.125 to 0.125
- w_up: bfloat16 [128, 768, 2048], P(('dp', 'expert'), 'tensor'), may hold values from -0.125 to 0.125
- w_down: bfloat16 [128, 768, 2048], P(('dp', 'expert'), 'tensor'), may hold values from -0.21875 to 0.21875
Outputs:
- grad_input: bfloat16 [16384, 2048], P(('dp', 'expert'), 'tensor')
- grad_gates: float32 [16384, 8], P(('dp', 'expert'))
The draws below stay inside these ranges and needn't reach their ends.
Inputs may be any that keep to these rules, and one draw needn't show every extreme that they name: `expert_ids`: each row names 8 different experts. Among the 128 rows of one device (aligned blocks of rows), no expert is named more than 8 times, a bound that some block reaches.
All inputs are finite; a program needn't handle non-finite values.
Results may differ from the reference program's by a relative error of at most 0.012.
Values may be sent and summed in bfloat16 or wider, within the bound.
A program may use at most 64 MiB of HBM per device.

```python
import math
import jax
import jax.numpy as jnp
import numpy as np
from jax import lax

D = 2048
FF = 768
TOP = 8
TOK_DEV = 128
EXPERTS = 128
CAP = 8
TOKENS = 16384
N_TENSOR = 4


def block_levels(rng, dims, cuts, smallest, high):
    factor_of, own = 1.0, jax.random.fold_in(rng, 6)
    for axis_at, parts in cuts:
        draws = jnp.exp(jax.random.uniform(jax.random.fold_in(own, axis_at), (parts,), jnp.float32, smallest / len(cuts), high / len(cuts)))
        factor_of = factor_of * jnp.repeat(draws, dims[axis_at] // parts).reshape([-1 if axis == axis_at else 1 for axis in range(len(dims))])
    return factor_of


def deal_out(own_key, own, number, rows, count, top, most, lean):
    order = jax.random.permutation(own_key, count)
    heavy_load, usual = portions_of(count, rows * top, most, lean, True), portions_of(count, rows * top, most, lean, False)
    places = jnp.arange(count)

    def named(sizes, turn):
        used = int((sizes > 0).sum())
        fixed = max(1, used // 4)
        passed = fixed + (places - fixed + turn * (used - fixed)) % max(1, count - fixed)
        return jnp.zeros((count,), jnp.int32).at[order[jnp.where(places < fixed, places, passed)]].set(jnp.asarray(sizes, jnp.int32))

    sizes = jnp.where(number % 4 == 0, named(heavy_load, number // 4), named(usual, number - number // 4 - 1))
    mixed = jax.random.permutation(jax.random.fold_in(own, 3), count)
    source_of, taker = mixed[0:count // 2 * 2:2], mixed[1:count // 2 * 2:2]
    room = jnp.minimum(sizes[source_of] - 1, most - sizes[taker]) // 2
    room = jnp.where((source_of == order[0]) | (taker == order[0]) | (sizes[taker] == 0), 0, jnp.maximum(room, 0))
    passed = jax.random.randint(jax.random.fold_in(own, 4), (count // 2,), 0, 1 << 20) % (room + 1)
    sizes = sizes.at[source_of].add(-passed).at[taker].add(passed)
    labels = jnp.searchsorted(jnp.cumsum(sizes), jnp.arange(rows * top), side="right").astype(jnp.int32)
    table = labels.reshape(top, rows).T
    table = table[jax.random.permutation(jax.random.fold_in(own, 1), rows)]
    turn = jax.random.randint(jax.random.fold_in(own, 2), (rows, 1), 0, top)
    return jnp.take_along_axis(table, (jnp.arange(top)[None, :] + turn) % top, axis=1)


def portions_of(number_of, total, limit, slope, full):
    loads = [(1 << 20) // math.isqrt(rank ** slope) + 1 for rank in range(1, number_of + 1)]
    largest = limit if full else min(limit, max(-(-total // number_of), total * loads[0] // sum(loads)))
    least = 1 if total - largest >= number_of - 1 else 0
    holding, surplus = [largest] + [least] * (number_of - 1), total - largest - least * (number_of - 1)
    while surplus > 0:
        movable = [i for i in range(1, number_of) if holding[i] < largest] or [i for i in range(1, number_of) if holding[i] < limit]
        whole, budget = sum([loads[i] for i in movable]), surplus
        for i in movable:
            extra = min(limit - holding[i], max(1, budget * loads[i] // whole), surplus)
            holding[i] = holding[i] + extra
            surplus = surplus - extra
    return np.array(holding)


def noise(rng, shape, width, most, shards=(), kind=jnp.bfloat16):
    gain = block_levels(rng, shape, shards, -0.22, 0.18) if shards else 1.0
    drawn = jax.random.normal(rng, shape, jnp.float32) * width * gain
    return jnp.minimum(jnp.maximum(drawn, -most), most).astype(kind)


def setup_inputs(seed: int = 0) -> dict:
    seeds = jax.random.split(jax.random.key(seed), 9)
    checkpoint = noise(seeds[0], (TOKENS, D), 1.0, 6.0, ((0, 128), (1, 4)))
    scales = jnp.clip(jnp.exp(math.log(2.0) - 1.3862944 * jax.random.uniform(seeds[1], (TOKENS,), jnp.float32) ** block_levels(seeds[1], (TOKENS,), ((0, 128),), -0.2, 0.2)), 0.5, 2.0)
    out_grad = noise(seeds[2], (TOKENS, D), 0.25, 1.5, ((0, 128), (1, 4)))
    expert_ids_keys = jax.random.split(jax.random.fold_in(seeds[3], 1), TOKENS // TOK_DEV)
    expert_ids_turns = jax.random.permutation(jax.random.fold_in(seeds[3], 3), TOKENS // TOK_DEV)
    expert_ids = jax.vmap(lambda own, number: deal_out(jax.random.fold_in(seeds[3], 2), own, number, TOK_DEV, EXPERTS, TOP, CAP, 0))(expert_ids_keys, expert_ids_turns).reshape((TOKENS, TOP))
    gates = jnp.clip(jnp.exp(math.log(1.0) - 2.9957323 * jax.random.uniform(seeds[4], (TOKENS, TOP), jnp.float32) ** block_levels(seeds[4], (TOKENS, TOP), ((0, 128),), -0.2, 0.2)), 0.05, 1.0)
    w_gate = noise(seeds[5], (EXPERTS, FF, D), D ** -0.5, 0.125, ((0, 128), (1, 4)))
    w_up = noise(seeds[6], (EXPERTS, FF, D), D ** -0.5, 0.125, ((0, 128), (1, 4)))
    w_down = noise(seeds[7], (EXPERTS, FF, D), FF ** -0.5, 0.21875, ((0, 128), (1, 4)))
    return {"checkpoint": checkpoint, "scales": scales, "out_grad": out_grad, "expert_ids": expert_ids, "gates": gates, "w_gate": w_gate, "w_up": w_up, "w_down": w_down}


def silu_parts(gate_pre, up_pre, back):
    sigma = jax.nn.sigmoid(gate_pre)
    swish = gate_pre * sigma
    hidden = (swish * up_pre).astype(jnp.bfloat16)
    d_gate = (back * up_pre * sigma * (1.0 + gate_pre * (1.0 - sigma))).astype(jnp.bfloat16)
    d_up = (back * swish).astype(jnp.bfloat16)
    return hidden, d_gate, d_up


def reference(checkpoint, scales, out_grad, expert_ids, gates, w_gate, w_up, w_down):
    dequant = (checkpoint.astype(jnp.float32) * scales[:, None]).astype(jnp.bfloat16)
    blocks = TOKENS // TOK_DEV
    pair_count = TOK_DEV * TOP
    block_ids = expert_ids.reshape(blocks, pair_count).astype(jnp.int32)
    onehot = (block_ids[:, :, None] == jnp.arange(EXPERTS, dtype=jnp.int32)[None, None, :]).astype(jnp.int32)
    earlier = jnp.cumsum(onehot, axis=1) - onehot
    position = jnp.sum(earlier * onehot, axis=2).astype(jnp.int32)
    column = jnp.arange(blocks, dtype=jnp.int32)[:, None] * CAP + position
    pair_index = jnp.arange(blocks * pair_count, dtype=jnp.int32).reshape(blocks, pair_count)
    table = jnp.full((EXPERTS, blocks * CAP), TOKENS * TOP, jnp.int32)
    table = table.at[block_ids.reshape(-1), column.reshape(-1)].set(pair_index.reshape(-1))
    gate_flat = gates.reshape(-1)
    quarter = FF // N_TENSOR
    slot_total = blocks * CAP
    contract = (((1,), (1,)), ((), ()))

    def per_expert(carry, inputs):
        grad_sum, gate_sum = carry
        pairs, weight_gate, weight_up, weight_down = inputs
        token_of = (pairs // TOP).astype(jnp.int32)
        rows_in = jnp.take(dequant, token_of, axis=0, mode="fill", fill_value=0)
        grads_in = jnp.take(out_grad, token_of, axis=0, mode="fill", fill_value=0)
        gate_pre = lax.dot_general(rows_in, weight_gate, contract, preferred_element_type=jnp.float32)
        up_pre = lax.dot_general(rows_in, weight_up, contract, preferred_element_type=jnp.float32)
        back = lax.dot_general(grads_in, weight_down, contract, preferred_element_type=jnp.float32)
        hidden, d_gate, d_up = silu_parts(gate_pre, up_pre, back)
        product = hidden.astype(jnp.float32) * back
        contrib = jnp.zeros((slot_total, D), jnp.float32)
        gate_term = jnp.zeros((slot_total,), jnp.float32)
        for rank in range(N_TENSOR):
            low = rank * quarter
            high = low + quarter
            part_sum = jnp.sum(product[:, low:high], axis=1).astype(jnp.bfloat16)
            gate_term = gate_term + lax.optimization_barrier(part_sum).astype(jnp.float32)
            piece = jnp.dot(d_gate[:, low:high], weight_gate[low:high, :], preferred_element_type=jnp.float32)
            piece = piece + jnp.dot(d_up[:, low:high], weight_up[low:high, :], preferred_element_type=jnp.float32)
            contrib = contrib + lax.optimization_barrier(piece.astype(jnp.bfloat16)).astype(jnp.float32)
        summed = lax.optimization_barrier(contrib.astype(jnp.bfloat16)).astype(jnp.float32)
        weight = jnp.take(gate_flat, pairs, mode="fill", fill_value=0)
        grad_sum = grad_sum.at[token_of].add(weight[:, None] * summed, mode="drop")
        gate_sum = gate_sum.at[pairs].add(gate_term, mode="drop")
        return (grad_sum, gate_sum), None

    start = (jnp.zeros((TOKENS, D), jnp.float32), jnp.zeros((TOKENS * TOP,), jnp.float32))
    (grad_sum, gate_sum), _ = lax.scan(per_expert, start, (table, w_gate, w_up, w_down))
    return grad_sum.astype(jnp.bfloat16), gate_sum.reshape(TOKENS, TOP)
```

```python
import jax
import jax.numpy as jnp
from jax import lax
from jax.sharding import PartitionSpec as P


def body(checkpoint, scales, out_grad, expert_ids, gates, w_gate, w_up, w_down):
    f32, bf16 = jnp.float32, jnp.bfloat16
    planes = lax.axis_size("tensor")
    experts = lax.axis_size("dp") * lax.axis_size("expert")
    rank = lax.axis_index("tensor")
    tokens, part = checkpoint.shape
    picks = expert_ids.shape[1]
    cap = tokens * picks // experts
    own = cap // planes
    width = part * planes
    wg = lax.all_gather(w_gate[0], "tensor", axis=0, tiled=True)
    wu = lax.all_gather(w_up[0], "tensor", axis=0, tiled=True)
    wd = lax.all_gather(w_down[0], "tensor", axis=0, tiled=True)
    dequant = (checkpoint.astype(f32) * scales[:, None]).astype(bf16)
    both = lax.all_gather(jnp.stack([dequant, out_grad]), "tensor", axis=2, tiled=True)

    named = expert_ids[:, :, None] == jnp.arange(experts, dtype=jnp.int32)[None, None, :]
    member = jnp.any(named, axis=1)
    weight = jnp.sum(jnp.where(named, gates[:, :, None], 0.0), axis=1)
    lower = (jnp.arange(tokens)[:, None] > jnp.arange(tokens)[None, :]).astype(bf16)
    place = jnp.dot(lower, member.astype(bf16), preferred_element_type=f32).astype(jnp.int32)
    slots = rank * own + jnp.arange(own, dtype=jnp.int32)
    pick = (member.T[:, None, :] & (place.T[:, None, :] == slots[None, :, None]))
    pick_rows = pick.reshape(experts * own, tokens)
    one = pick_rows.astype(bf16)
    send_x = jnp.dot(one, both[0], preferred_element_type=f32).astype(bf16)
    send_g = jnp.dot(one, both[1], preferred_element_type=f32).astype(bf16)
    names = ("dp", "expert")
    rows = lax.all_to_all(send_x.reshape(experts, own, width), names, 0, 0, tiled=True)
    grads = lax.all_to_all(send_g.reshape(experts, own, width), names, 0, 0, tiled=True)
    rows = rows.reshape(experts * own, width)
    grads = grads.reshape(experts * own, width)
    contract = (((1,), (1,)), ((), ()))
    gate_pre = lax.dot_general(rows, wg, contract, preferred_element_type=f32)
    up_pre = lax.dot_general(rows, wu, contract, preferred_element_type=f32)
    back = lax.dot_general(grads, wd, contract, preferred_element_type=f32)
    sigma = jax.nn.sigmoid(gate_pre)
    swish = gate_pre * sigma
    hidden = (swish * up_pre).astype(bf16)
    gate_term = jnp.sum(hidden.astype(f32) * back, axis=1)
    d_gate = (back * up_pre * sigma * (1.0 + gate_pre * (1.0 - sigma))).astype(bf16)
    d_up = (back * swish).astype(bf16)
    result = jnp.dot(d_gate, wg, preferred_element_type=f32)
    result = result + jnp.dot(d_up, wu, preferred_element_type=f32)
    tail = jnp.broadcast_to(gate_term[:, None], (experts * own, 128))
    packed = jnp.concatenate([result.astype(bf16), tail.astype(bf16)], axis=1)
    came = lax.all_to_all(packed.reshape(experts, own, width + 128), names, 0, 0, tiled=True)
    came = came.reshape(experts * own, width + 128)
    combine = jnp.where(pick, weight.T[:, None, :], 0.0).reshape(experts * own, tokens)
    high = combine.astype(bf16)
    low = (combine - high.astype(f32)).astype(bf16)
    flip = (((0,), (0,)), ((), ()))
    mixed = lax.dot_general(high, came[:, :width], flip, preferred_element_type=f32)
    mixed = mixed + lax.dot_general(low, came[:, :width], flip, preferred_element_type=f32)
    term = jnp.sum(jnp.where(pick, came[:, width].astype(f32).reshape(experts, own)[:, :, None], 0.0), axis=1)
    terms = jnp.sum(jnp.where(named, term.T[:, None, :], 0.0), axis=2)
    terms = jnp.pad(terms, ((0, 0), (0, 128 - picks))).astype(bf16)
    joined = jnp.concatenate(
        [mixed.astype(bf16).reshape(tokens, planes, part), jnp.broadcast_to(terms[:, None], (tokens, planes, 128))],
        axis=2,
    ).transpose(1, 0, 2)
    summed = lax.psum_scatter(joined, "tensor", scatter_dimension=0, tiled=True)[0]
    return summed[:, :part], summed[:, part : part + picks].astype(f32)


def solution(mesh):
    return jax.shard_map(
        body,
        mesh=mesh,
        in_specs=(
            P(("dp", "expert"), "tensor"),
            P(("dp", "expert")),
            P(("dp", "expert"), "tensor"),
            P(("dp", "expert"), None),
            P(("dp", "expert"), None),
            P(("dp", "expert"), "tensor", None),
            P(("dp", "expert"), "tensor", None),
            P(("dp", "expert"), "tensor", None),
        ),
        out_specs=(P(("dp", "expert"), "tensor"), P(("dp", "expert"), None)),
        check_vma=False,
    )
```

```python
import functools

import jax
import jax.numpy as jnp
from jax import lax
from jax.experimental import pallas as pl
from jax.experimental.pallas import tpu as pltpu
from jax.sharding import PartitionSpec as P

F32, BF16 = jnp.float32, jnp.bfloat16
NT = (((1,), (1,)), ((), ()))


def kernel(
    ny,
    nz,
    ids,
    gates,
    scales,
    ck,
    og,
    wg,
    wu,
    wd,
    out,
    terms_out,
    raw,
    xd,
    hot,
    mix_hi,
    mix_lo,
    sendb,
    rows,
    w,
    psend,
    pin,
    keep,
    ret,
    came,
    fin32,
    fin16,
    fin_in,
    part_t,
    gather_t,
    loc_sem,
    a_send,
    a_recv,
    w_send,
    w_recv,
    d_send,
    d_recv,
    b_send,
    b_recv,
    p_send,
    p_recv,
    r_send,
    r_recv,
    f_send,
    f_recv,
    t_send,
    t_recv,
):
    n_chunk = keep.shape[0]
    per = ny // n_chunk
    cap = sendb.shape[3]
    half = sendb.shape[4]
    part = half // 2
    picks, tokens = ids.shape
    dp = lax.axis_index("dp")
    x = lax.axis_index("tensor")
    chip = lax.axis_index("expert")
    yy, zz = chip // nz, chip % nz
    h = x // 2
    a = (x + x // 2) % 2
    me = x % 2
    mate = 1 - me
    core = (dp + a) % 2
    a_peer = {"tensor": 2 * h + mate}
    b_peer = {"tensor": 3 - x}

    def turn(j):
        if ny == 8:
            return (j % 2) * 4 + ((j // 2) % 2) * 2 + j // 4
        return j

    def target(j, dz):
        return {"dp": core, "expert": ((yy + turn(j)) % ny) * nz + (zz + dz) % nz}

    def origin(j, dz):
        return {"dp": core, "expert": ((yy + ny - turn(j)) % ny) * nz + (zz + nz - dz) % nz}

    def for_all(j, dz, act):
        @pl.when((a == 1) | (j * nz + dz > 0))
        def _():
            act()

    weights = (wg, wu, wd)
    local = [
        pltpu.make_async_copy(ck, raw.at[me, 0], loc_sem.at[0]),
        pltpu.make_async_copy(og, raw.at[me, 1], loc_sem.at[1]),
    ]
    for m in range(3):
        for f in range(2):
            local.append(
                pltpu.make_async_copy(
                    weights[m].at[:, pl.ds(f * half, half)], w.at[m, me, f], loc_sem.at[2 + 2 * m + f]
                )
            )
    for copy in local:
        copy.start()

    barrier = pltpu.get_barrier_semaphore()
    for step in range(1, 4):
        pl.semaphore_signal(barrier, inc=1, device_id={"tensor": (x + step) % 4})

    def greet(j, carry):
        for dz in range(nz):
            for_all(j, dz, lambda: pl.semaphore_signal(barrier, inc=1, device_id=target(j, dz)))
        return carry

    lax.fori_loop(0, ny, greet, 0)

    r = lax.broadcasted_iota(jnp.int32, (ny * nz, tokens), 0)
    rj, rz = r // nz, r % nz
    expert = core * (ny * nz) + ((yy + turn(rj)) % ny) * nz + (zz + rz) % nz
    member = jnp.zeros((ny * nz, tokens), F32)
    gate = jnp.zeros((ny * nz, tokens), F32)
    for k in range(picks):
        same = ids[pl.ds(k, 1), :] == expert
        member = jnp.where(same, 1.0, member)
        gate = jnp.where(same, gates[pl.ds(k, 1), :], gate)
    before = lax.broadcasted_iota(jnp.int32, (tokens, tokens), 0) < lax.broadcasted_iota(
        jnp.int32, (tokens, tokens), 1
    )
    place = jnp.dot(member.astype(BF16), before.astype(F32).astype(BF16), preferred_element_type=F32)
    slot = lax.broadcasted_iota(jnp.int32, (ny * nz, cap, tokens), 1).astype(F32)
    place = jnp.where(member > 0.0, place, -1.0)
    pick = jnp.where(place[:, None, :] == slot, 1.0, 0.0)
    hot[...] = pick.reshape(ny, nz * cap, tokens).astype(BF16)
    mix = (pick * gate[:, None, :]).reshape(ny * nz * cap, tokens).T
    high = mix.astype(BF16)
    mix_hi[...] = high
    mix_lo[...] = (mix - high.astype(F32)).astype(BF16)

    pl.semaphore_wait(barrier, ny * nz + 2 + a)

    def remote(src, dst, send, recv, where):
        return pltpu.make_async_remote_copy(
            src_ref=src, dst_ref=dst, send_sem=send, recv_sem=recv, device_id=where
        )

    a_copies = [
        remote(ck, raw.at[me, 0], a_send.at[0], a_recv.at[0], a_peer),
        remote(og, raw.at[me, 1], a_send.at[1], a_recv.at[1], a_peer),
    ]
    for m in range(3):
        for f in range(2):
            a_copies.append(
                remote(
                    weights[m].at[:, pl.ds(f * half, half)],
                    w.at[m, me, f],
                    w_send.at[2 * m + f],
                    w_recv.at[2 * m + f],
                    a_peer,
                )
            )
    for copy in a_copies:
        copy.start()
    for i in range(2):
        local[i].wait()
    for i in range(2):
        remote(ck, raw.at[mate, i], a_send.at[i], a_recv.at[i], a_peer).wait_recv()

    for q in range(2):
        xd[q, 0] = (raw[q, 0].astype(F32) * scales[...]).astype(BF16)
        xd[q, 1] = raw[q, 1]

    def dispatch(j, carry):
        chosen = hot[j]
        for i in range(2):
            for q in range(2):
                got = jnp.dot(chosen, xd[q, i], preferred_element_type=F32)
                sendb[j, :, i, :, q * part : (q + 1) * part] = got.reshape(nz, cap, part).astype(BF16)
        for dz in range(nz):
            for_all(
                j,
                dz,
                lambda: remote(
                    sendb.at[j, dz], rows.at[h, j, dz], d_send.at[j], d_recv.at[j], target(j, dz)
                ).start(),
            )
        return carry

    lax.fori_loop(0, ny, dispatch, 0)

    @pl.when(a == 0)
    def _():
        rows[h, 0, 0] = sendb[0, 0]

    def all_but_own(j, ref, wait):
        @pl.when((a == 1) | (j > 0))
        def _():
            wait(ref)

        if nz > 1:

            @pl.when((a == 0) & (j == 0))
            def _():
                wait(ref.at[pl.ds(1, nz - 1)])

    def forward(j, carry):
        all_but_own(
            j,
            rows.at[h, j],
            lambda ref: remote(ref, ref, d_send.at[j], d_recv.at[j], b_peer).wait_recv(),
        )
        remote(rows.at[h, j], rows.at[h, j], b_send.at[j], b_recv.at[j], b_peer).start()
        return carry

    lax.fori_loop(0, ny, forward, 0)

    for i in range(2, 8):
        local[i].wait()
    for m in range(3):
        for f in range(2):
            remote(
                w.at[m, mate, f], w.at[m, mate, f], w_send.at[2 * m + f], w_recv.at[2 * m + f], a_peer
            ).wait_recv()

    n_rows = per * nz * cap

    def flat(ref):
        value = ref[...].astype(F32)
        return value.reshape(n_rows, value.shape[-1]).astype(BF16)

    def matrix(m, f):
        value = w[m, :, f]
        return value.reshape(2 * value.shape[1], half)

    def compute(c, carry):
        def arrived(i, carry):
            j = c * per + i
            other = rows.at[1 - h, j]
            remote(other, other, b_send.at[j], b_recv.at[j], b_peer).wait_recv()
            return carry

        lax.fori_loop(0, per, arrived, 0)
        first = c * per
        gate_pre = up_pre = back = 0.0
        for f in range(2):
            mine = flat(rows.at[f, pl.ds(first, per), :, 0])
            grad = flat(rows.at[f, pl.ds(first, per), :, 1])
            gate_pre += lax.dot_general(mine, matrix(0, f), NT, preferred_element_type=F32)
            up_pre += lax.dot_general(mine, matrix(1, f), NT, preferred_element_type=F32)
            back += lax.dot_general(grad, matrix(2, f), NT, preferred_element_type=F32)
        sigma = jax.nn.sigmoid(gate_pre)
        swish = gate_pre * sigma
        hidden = (swish * up_pre).astype(BF16)
        term = jnp.sum(hidden.astype(F32) * back, axis=1, keepdims=True)
        d_gate = (back * up_pre * sigma * (1.0 + gate_pre * (1.0 - sigma))).astype(BF16)
        d_up = (back * swish).astype(BF16)
        for which in range(2):
            f = h if which else 1 - h
            result = jnp.dot(d_gate, matrix(0, f), preferred_element_type=F32)
            result = result + jnp.dot(d_up, matrix(1, f), preferred_element_type=F32)
            if which:
                keep[c] = result
            else:
                psend[c] = result.astype(BF16)
                remote(psend.at[c], pin.at[c], p_send.at[c], p_recv.at[c], b_peer).start()
        wide = jnp.broadcast_to(term, (n_rows, 128)).reshape(per, nz, cap, 128).astype(BF16)
        ret[pl.ds(first, per), :, :, pl.ds(half, 128)] = wide
        return carry

    lax.fori_loop(0, n_chunk, compute, 0)

    def give_back(c, carry):
        first = c * per
        remote(psend.at[c], pin.at[c], p_send.at[c], p_recv.at[c], b_peer).wait_recv()
        total = keep[c] + pin[c].astype(F32)
        ret[pl.ds(first, per), :, :, pl.ds(0, half)] = total.reshape(per, nz, cap, half).astype(BF16)

        def one(i, carry):
            j = first + i
            for dz in range(nz):
                for_all(
                    j,
                    dz,
                    lambda: remote(
                        ret.at[j, dz], came.at[j, dz], r_send.at[j], r_recv.at[j], origin(j, dz)
                    ).start(),
                )
            return carry

        lax.fori_loop(0, per, one, 0)
        return carry

    lax.fori_loop(0, n_chunk, give_back, 0)

    @pl.when(a == 0)
    def _():
        came[0, 0] = ret[0, 0]

    def landed(j, carry):
        all_but_own(
            j,
            came.at[j],
            lambda ref: remote(ref, ref, r_send.at[j], r_recv.at[j], b_peer).wait_recv(),
        )
        return carry

    lax.fori_loop(0, ny, landed, 0)
    back_rows = came[:, :, :, pl.ds(0, half)].astype(F32).reshape(ny * nz * cap, half).astype(BF16)
    mixed = jnp.dot(mix_hi[...], back_rows, preferred_element_type=F32)
    mixed = mixed + jnp.dot(mix_lo[...], back_rows, preferred_element_type=F32)
    for q in range(2):
        fin32[q] = mixed[:, q * part : (q + 1) * part]
        fin16[q] = mixed[:, q * part : (q + 1) * part].astype(BF16)
    last = remote(fin16.at[mate], fin_in, f_send.at[0], f_recv.at[0], a_peer)
    last.start()

    seen = came[:, :, :, pl.ds(half, 128)].astype(F32).reshape(ny * nz, cap, 128)[:, :, :tokens]
    chosen = hot[...].astype(F32).reshape(ny * nz, cap, tokens)
    by_expert = jnp.sum(chosen * seen, axis=1)
    lines = []
    for k in range(picks):
        same = ids[pl.ds(k, 1), :] == expert
        lines.append(jnp.sum(jnp.where(same, by_expert, 0.0), axis=0, keepdims=True))
    own = jnp.concatenate(lines, axis=0)
    part_t[...] = own
    sends = []
    for step in range(1, 4):
        sends.append(
            remote(
                part_t,
                gather_t.at[step - 1],
                t_send.at[step - 1],
                t_recv.at[step - 1],
                {"tensor": (x + step) % 4},
            )
        )
        sends[-1].start()
    last.wait()
    out[...] = (fin32[me] + fin_in[...].astype(F32)).astype(BF16)
    for copy in sends:
        copy.wait()
    terms_out[...] = own + gather_t[0] + gather_t[1] + gather_t[2]

    for copy in a_copies:
        copy.wait_send()

    def drain(j, carry):
        all_but_own(
            j, sendb.at[j], lambda ref: remote(ref, ref, d_send.at[j], d_recv.at[j], b_peer).wait_send()
        )
        remote(rows.at[h, j], rows.at[h, j], b_send.at[j], b_recv.at[j], b_peer).wait_send()
        all_but_own(
            j, ret.at[j], lambda ref: remote(ref, ref, r_send.at[j], r_recv.at[j], b_peer).wait_send()
        )
        return carry

    lax.fori_loop(0, ny, drain, 0)
    for c in range(n_chunk):
        remote(psend.at[c], pin.at[c], p_send.at[c], p_recv.at[c], b_peer).wait_send()


def body(ny, nz, checkpoint, scales, out_grad, expert_ids, gates, w_gate, w_up, w_down):
    tokens, part = checkpoint.shape
    picks = expert_ids.shape[1]
    cap = tokens * picks // (2 * ny * nz)
    hidden = w_gate.shape[1]
    half = 2 * part
    n_chunk = 2
    n_rows = ny * nz * cap
    chunk = n_rows // n_chunk
    dma = pltpu.SemaphoreType.DMA
    vmem = pl.BlockSpec(memory_space=pltpu.VMEM)
    anyw = pl.BlockSpec(memory_space=pl.ANY)
    out, terms = pl.pallas_call(
        functools.partial(kernel, ny, nz),
        name="experts",
        out_shape=(
            jax.ShapeDtypeStruct((tokens, part), BF16),
            jax.ShapeDtypeStruct((picks, tokens), F32),
        ),
        in_specs=[vmem, vmem, vmem] + [anyw] * 5,
        out_specs=(vmem, vmem),
        scratch_shapes=[
            pltpu.VMEM((2, 2, tokens, part), BF16),
            pltpu.VMEM((2, 2, tokens, part), BF16),
            pltpu.VMEM((ny, nz * cap, tokens), BF16),
            pltpu.VMEM((tokens, n_rows), BF16),
            pltpu.VMEM((tokens, n_rows), BF16),
            pltpu.VMEM((ny, nz, 2, cap, half), BF16),
            pltpu.VMEM((2, ny, nz, 2, cap, half), BF16),
            pltpu.VMEM((3, 2, 2, hidden, half), BF16),
            pltpu.VMEM((n_chunk, chunk, half), BF16),
            pltpu.VMEM((n_chunk, chunk, half), BF16),
            pltpu.VMEM((n_chunk, chunk, half), F32),
            pltpu.VMEM((ny, nz, cap, half + 128), BF16),
            pltpu.VMEM((ny, nz, cap, half + 128), BF16),
            pltpu.VMEM((2, tokens, part), F32),
            pltpu.VMEM((2, tokens, part), BF16),
            pltpu.VMEM((tokens, part), BF16),
            pltpu.VMEM((picks, tokens), F32),
            pltpu.VMEM((3, picks, tokens), F32),
            dma((8,)),
            dma((2,)),
            dma((2,)),
            dma((6,)),
            dma((6,)),
            dma((ny,)),
            dma((ny,)),
            dma((ny,)),
            dma((ny,)),
            dma((n_chunk,)),
            dma((n_chunk,)),
            dma((ny,)),
            dma((ny,)),
            dma((1,)),
            dma((1,)),
            dma((3,)),
            dma((3,)),
        ],
        compiler_params=pltpu.CompilerParams(
            collective_id=0, has_side_effects=True, vmem_limit_bytes=60 * 1024 * 1024
        ),
    )(
        expert_ids.T,
        gates.T,
        scales[:, None],
        checkpoint,
        out_grad,
        w_gate[0],
        w_up[0],
        w_down[0],
    )
    return out, terms.T


def solution(mesh):
    n = mesh.shape["expert"]
    ny = 8 if n == 64 else n
    return jax.shard_map(
        functools.partial(body, ny, n // ny),
        mesh=mesh,
        in_specs=(
            P(("dp", "expert"), "tensor"),
            P(("dp", "expert")),
            P(("dp", "expert"), "tensor"),
            P(("dp", "expert"), None),
            P(("dp", "expert"), None),
            P(("dp", "expert"), "tensor", None),
            P(("dp", "expert"), "tensor", None),
            P(("dp", "expert"), "tensor", None),
        ),
        out_specs=(P(("dp", "expert"), "tensor"), P(("dp", "expert"), None)),
        check_vma=False,
    )
```

```python
import functools

import jax
import jax.numpy as jnp
from jax import lax
from jax.experimental import pallas as pl
from jax.experimental.pallas import tpu as pltpu
from jax.sharding import PartitionSpec as P

F32, BF16 = jnp.float32, jnp.bfloat16
NT = (((1,), (1,)), ((), ()))


def send_order(ny, nz):
    def far(step):
        return min(step[0], ny - step[0]) + min(step[1], nz - step[1])

    steps = sorted(((y, z) for y in range(ny) for z in range(nz)), key=far)
    order = []
    for y, z in steps:
        images = [(y, z), (-y, -z), (y, -z), (-y, z)]
        if ny == nz:
            images = [(y, z), (-y, -z), (z, -y), (-z, y), (y, -z), (-y, z), (z, y), (-z, -y)]
        for u, v in images:
            if (u % ny, v % nz) not in order:
                order.append((u % ny, v % nz))
    return order


def kernel(
    ny,
    nz,
    ids,
    gates,
    scales,
    ck,
    og,
    wg,
    wu,
    wd,
    out,
    terms_out,
    raw,
    hot,
    mix_hi,
    mix_lo,
    sendb,
    rows,
    w,
    psend,
    pin,
    keep,
    ret,
    came,
    fin32,
    fin16,
    fin_in,
    part_t,
    gather_t,
    loc_sem,
    a_send,
    a_recv,
    w_send,
    w_recv,
    d_send,
    d_recv,
    b_send,
    b_recv,
    p_send,
    p_recv,
    r_send,
    r_recv,
    f_send,
    f_recv,
    t_send,
    t_recv,
):
    order = send_order(ny, nz)
    peers = ny * nz
    groups = keep.shape[0]
    per = peers // groups
    cap, part = sendb.shape[3:]
    half = 2 * part
    picks, tokens = ids.shape
    dp = lax.axis_index("dp")
    x = lax.axis_index("tensor")
    chip = lax.axis_index("expert")
    yy, zz = chip // nz, chip % nz
    h = x // 2
    a = (x + x // 2) % 2
    me = x % 2
    mate = 1 - me
    core = (dp + a) % 2
    a_peer = {"tensor": 2 * h + mate}
    b_peer = {"tensor": 3 - x}
    to_y = [((yy + d) % ny) * nz for d in range(ny)]
    to_z = [(zz + d) % nz for d in range(nz)]

    def target(n):
        y, z = order[n]
        return {"dp": core, "expert": to_y[y] + to_z[z]}

    def origin(n):
        y, z = order[n]
        return {"dp": core, "expert": to_y[-y % ny] + to_z[-z % nz]}

    def each(first, count, act):
        for n in range(first, first + count):
            if n == 0:
                pl.when(a == 1)(functools.partial(act, n))
            else:
                act(n)

    def remote(src, dst, send, recv, where):
        return pltpu.make_async_remote_copy(
            src_ref=src, dst_ref=dst, send_sem=send, recv_sem=recv, device_id=where
        )

    def one_wait(g, ref, wait):
        @pl.when((a == 1) | (g > 0))
        def _():
            wait(ref.at[pl.ds(g * per, per)])

        if per > 1:

            @pl.when((a == 0) & (g == 0))
            def _():
                wait(ref.at[pl.ds(1, per - 1)])

    weights = (wg, wu, wd)
    local = [
        pltpu.make_async_copy(ck, raw.at[me, 0], loc_sem.at[0]),
        pltpu.make_async_copy(og, raw.at[me, 1], loc_sem.at[1]),
    ]
    for m in range(3):
        for f in range(2):
            local.append(
                pltpu.make_async_copy(
                    weights[m].at[:, pl.ds(f * half, half)], w.at[m, me, f], loc_sem.at[2 + 2 * m + f]
                )
            )
    for copy in local:
        copy.start()

    barrier = pltpu.get_barrier_semaphore()
    for step in range(1, 4):
        pl.semaphore_signal(barrier, inc=1, device_id={"tensor": (x + step) % 4})
    each(0, peers, lambda n: pl.semaphore_signal(barrier, inc=1, device_id=target(n)))

    r = lax.broadcasted_iota(jnp.int32, (peers, tokens), 0)
    expert = jnp.zeros((peers, tokens), jnp.int32)
    for n in range(peers):
        y, z = order[n]
        expert = jnp.where(r == n, core * peers + to_y[y] + to_z[z], expert)
    member = jnp.zeros((peers, tokens), F32)
    gate = jnp.zeros((peers, tokens), F32)
    for k in range(picks):
        same = ids[pl.ds(k, 1), :] == expert
        member = jnp.where(same, 1.0, member)
        gate = jnp.where(same, gates[pl.ds(k, 1), :], gate)
    before = lax.broadcasted_iota(jnp.int32, (tokens, tokens), 0) < lax.broadcasted_iota(
        jnp.int32, (tokens, tokens), 1
    )
    place = jnp.dot(member.astype(BF16), before.astype(F32).astype(BF16), preferred_element_type=F32)
    slot = lax.broadcasted_iota(jnp.int32, (peers, cap, tokens), 1).astype(F32)
    place = jnp.where(member > 0.0, place, -1.0)
    pick = jnp.where(place[:, None, :] == slot, 1.0, 0.0)
    hot[...] = pick.reshape(groups, per * cap, tokens).astype(BF16)
    mix = (pick * gate[:, None, :]).reshape(peers * cap, tokens).T
    high = mix.astype(BF16)
    mix_hi[...] = high
    mix_lo[...] = (mix - high.astype(F32)).astype(BF16)

    def build(q):
        sources = ((raw[q, 0].astype(F32) * scales[...]).astype(BF16), raw[q, 1])

        def group(g, carry):
            chosen = hot[g]
            for i in range(2):
                got = jnp.dot(chosen, sources[i], preferred_element_type=F32)
                sendb[q, pl.ds(g * per, per), i] = got.reshape(per, cap, part).astype(BF16)
            return carry

        lax.fori_loop(0, groups, group, 0)

        @pl.when(a == 0)
        def _():
            rows[2 * h + q, 0] = sendb[q, 0]

    def dispatch(q, turn):
        each(
            0,
            peers,
            lambda n: remote(
                sendb.at[q, n],
                rows.at[2 * h + q, n],
                d_send.at[turn, n // per],
                d_recv.at[turn, n // per],
                target(n),
            ).start(),
        )

    def forward(q, turn):
        def group(g, carry):
            one_wait(
                g,
                rows.at[2 * h + q],
                lambda ref: remote(ref, ref, d_send.at[turn, g], d_recv.at[turn, g], b_peer).wait_recv(),
            )
            ref = rows.at[2 * h + q, pl.ds(g * per, per)]
            remote(ref, ref, b_send.at[turn, g], b_recv.at[turn, g], b_peer).start()
            return carry

        lax.fori_loop(0, groups, group, 0)

    for i in range(2):
        local[i].wait()
    build(me)
    pl.semaphore_wait(barrier, peers + 2 + a)

    a_copies = [
        remote(ck, raw.at[me, 0], a_send.at[0], a_recv.at[0], a_peer),
        remote(og, raw.at[me, 1], a_send.at[1], a_recv.at[1], a_peer),
    ]
    for m in range(3):
        for f in range(2):
            a_copies.append(
                remote(
                    weights[m].at[:, pl.ds(f * half, half)],
                    w.at[m, me, f],
                    w_send.at[2 * m + f],
                    w_recv.at[2 * m + f],
                    a_peer,
                )
            )
    for copy in a_copies:
        copy.start()
    dispatch(me, 0)
    for i in range(2):
        remote(ck, raw.at[mate, i], a_send.at[i], a_recv.at[i], a_peer).wait_recv()
    build(mate)
    dispatch(mate, 1)
    forward(me, 0)
    forward(mate, 1)

    for i in range(2, 8):
        local[i].wait()
    for m in range(3):
        for f in range(2):
            remote(
                w.at[m, mate, f], w.at[m, mate, f], w_send.at[2 * m + f], w_recv.at[2 * m + f], a_peer
            ).wait_recv()

    wide = max(1, groups // 4)
    steps = groups // wide
    n_rows = wide * per * cap

    def give_back(g):
        remote(psend.at[g], pin.at[g], p_send.at[g], p_recv.at[g], b_peer).wait_recv()
        total = keep[g] + pin[g].astype(F32)
        ret[pl.ds(g * per, per), :, pl.ds(0, half)] = total.reshape(per, cap, half).astype(BF16)
        each(
            g * per,
            per,
            lambda n: remote(ret.at[n], came.at[n], r_send.at[g], r_recv.at[g], origin(n)).start(),
        )

    def compute(c, carry):
        first = c * wide
        for i in range(wide):
            other = rows.at[0, pl.ds((first + i) * per, per)]
            for turn in range(2):
                remote(
                    other, other, b_send.at[turn, first + i], b_recv.at[turn, first + i], b_peer
                ).wait_recv()
        gate_pre = up_pre = back = 0.0
        for fq in range(4):
            lanes = slice((fq % 2) * part, (fq % 2 + 1) * part)

            def matrix(m):
                value = w[m, :, fq // 2, :, lanes]
                return value.reshape(2 * value.shape[1], part)

            def flat(i):
                value = rows[fq, pl.ds(first * per, wide * per), i].astype(F32)
                return value.reshape(n_rows, part).astype(BF16)

            mine, grad = flat(0), flat(1)
            gate_pre += lax.dot_general(mine, matrix(0), NT, preferred_element_type=F32)
            up_pre += lax.dot_general(mine, matrix(1), NT, preferred_element_type=F32)
            back += lax.dot_general(grad, matrix(2), NT, preferred_element_type=F32)
        sigma = jax.nn.sigmoid(gate_pre)
        swish = gate_pre * sigma
        hidden = (swish * up_pre).astype(BF16)
        term = jnp.sum(hidden.astype(F32) * back, axis=1, keepdims=True)
        d_gate = (back * up_pre * sigma * (1.0 + gate_pre * (1.0 - sigma))).astype(BF16)
        d_up = (back * swish).astype(BF16)
        for own in range(2):
            f = h if own else 1 - h
            down_g, down_u = (w[m, :, f].reshape(2 * w.shape[3], half) for m in range(2))
            result = jnp.dot(d_gate, down_g, preferred_element_type=F32)
            result = result + jnp.dot(d_up, down_u, preferred_element_type=F32)
            result = result.reshape(wide, per * cap, half)
            if own:
                keep[pl.ds(first, wide)] = result
            else:
                psend[pl.ds(first, wide)] = result.astype(BF16)
                for i in range(wide):
                    g = first + i
                    remote(psend.at[g], pin.at[g], p_send.at[g], p_recv.at[g], b_peer).start()
        spread = jnp.broadcast_to(term, (n_rows, 128)).reshape(wide * per, cap, 128).astype(BF16)
        ret[pl.ds(first * per, wide * per), :, pl.ds(half, 128)] = spread
        for early in range(steps - 2):
            pl.when(c == early + 1)(functools.partial(give_back, early))
        return carry

    lax.fori_loop(0, steps, compute, 0)
    for g in range(max(0, steps - 2), groups):
        give_back(g)

    @pl.when(a == 0)
    def _():
        came[0] = ret[0]

    def landed(g, carry):
        one_wait(
            g, came, lambda ref: remote(ref, ref, r_send.at[g], r_recv.at[g], b_peer).wait_recv()
        )
        return carry

    lax.fori_loop(0, groups, landed, 0)
    back_rows = came[:, :, pl.ds(0, half)].astype(F32).reshape(peers * cap, half).astype(BF16)
    mixed = jnp.dot(mix_hi[...], back_rows, preferred_element_type=F32)
    mixed = mixed + jnp.dot(mix_lo[...], back_rows, preferred_element_type=F32)
    for q in range(2):
        fin32[q] = mixed[:, q * part : (q + 1) * part]
        fin16[q] = mixed[:, q * part : (q + 1) * part].astype(BF16)
    last = remote(fin16.at[mate], fin_in, f_send.at[0], f_recv.at[0], a_peer)
    last.start()

    seen = came[:, :, pl.ds(half, 128)].astype(F32)[:, :, :tokens]
    chosen = hot[...].astype(F32).reshape(peers, cap, tokens)
    by_expert = jnp.sum(chosen * seen, axis=1)
    lines = []
    for k in range(picks):
        same = ids[pl.ds(k, 1), :] == expert
        lines.append(jnp.sum(jnp.where(same, by_expert, 0.0), axis=0, keepdims=True))
    own = jnp.concatenate(lines, axis=0)
    part_t[...] = own
    sends = []
    for step in range(1, 4):
        sends.append(
            remote(
                part_t,
                gather_t.at[step - 1],
                t_send.at[step - 1],
                t_recv.at[step - 1],
                {"tensor": (x + step) % 4},
            )
        )
        sends[-1].start()
    last.wait()
    out[...] = (fin32[me] + fin_in[...].astype(F32)).astype(BF16)
    for copy in sends:
        copy.wait()
    terms_out[...] = own + gather_t[0] + gather_t[1] + gather_t[2]

    for copy in a_copies:
        copy.wait_send()

    def drain(g, carry):
        for turn, q in enumerate((me, mate)):
            one_wait(
                g,
                sendb.at[q],
                lambda ref: remote(ref, ref, d_send.at[turn, g], d_recv.at[turn, g], b_peer).wait_send(),
            )
            ref = rows.at[2 * h + q, pl.ds(g * per, per)]
            remote(ref, ref, b_send.at[turn, g], b_recv.at[turn, g], b_peer).wait_send()
        one_wait(
            g, ret, lambda ref: remote(ref, ref, r_send.at[g], r_recv.at[g], b_peer).wait_send()
        )
        remote(psend.at[g], pin.at[g], p_send.at[g], p_recv.at[g], b_peer).wait_send()
        return carry

    lax.fori_loop(0, groups, drain, 0)


def body(ny, nz, checkpoint, scales, out_grad, expert_ids, gates, w_gate, w_up, w_down):
    tokens, part = checkpoint.shape
    picks = expert_ids.shape[1]
    peers = ny * nz
    cap = tokens * picks // (2 * peers)
    hidden = w_gate.shape[1]
    half = 2 * part
    groups = max(2, peers // 8)
    group_rows = peers * cap // groups
    dma = pltpu.SemaphoreType.DMA
    vmem = pl.BlockSpec(memory_space=pltpu.VMEM)
    anyw = pl.BlockSpec(memory_space=pl.ANY)
    out, terms = pl.pallas_call(
        functools.partial(kernel, ny, nz),
        name="experts",
        out_shape=(
            jax.ShapeDtypeStruct((tokens, part), BF16),
            jax.ShapeDtypeStruct((picks, tokens), F32),
        ),
        in_specs=[vmem, vmem, vmem] + [anyw] * 5,
        out_specs=(vmem, vmem),
        scratch_shapes=[
            pltpu.VMEM((2, 2, tokens, part), BF16),
            pltpu.VMEM((groups, group_rows, tokens), BF16),
            pltpu.VMEM((tokens, peers * cap), BF16),
            pltpu.VMEM((tokens, peers * cap), BF16),
            pltpu.VMEM((2, peers, 2, cap, part), BF16),
            pltpu.VMEM((4, peers, 2, cap, part), BF16),
            pltpu.VMEM((3, 2, 2, hidden, half), BF16),
            pltpu.VMEM((groups, group_rows, half), BF16),
            pltpu.VMEM((groups, group_rows, half), BF16),
            pltpu.VMEM((groups, group_rows, half), F32),
            pltpu.VMEM((peers, cap, half + 128), BF16),
            pltpu.VMEM((peers, cap, half + 128), BF16),
            pltpu.VMEM((2, tokens, part), F32),
            pltpu.VMEM((2, tokens, part), BF16),
            pltpu.VMEM((tokens, part), BF16),
            pltpu.VMEM((picks, tokens), F32),
            pltpu.VMEM((3, picks, tokens), F32),
            dma((8,)),
            dma((2,)),
            dma((2,)),
            dma((6,)),
            dma((6,)),
            dma((2, groups)),
            dma((2, groups)),
            dma((2, groups)),
            dma((2, groups)),
            dma((groups,)),
            dma((groups,)),
            dma((groups,)),
            dma((groups,)),
            dma((1,)),
            dma((1,)),
            dma((3,)),
            dma((3,)),
        ],
        compiler_params=pltpu.CompilerParams(
            collective_id=0, has_side_effects=True, vmem_limit_bytes=60 * 1024 * 1024
        ),
    )(
        expert_ids.T,
        gates.T,
        scales[:, None],
        checkpoint,
        out_grad,
        w_gate[0],
        w_up[0],
        w_down[0],
    )
    return out, terms.T


def solution(mesh):
    n = mesh.shape["expert"]
    ny = 8 if n == 64 else n
    return jax.shard_map(
        functools.partial(body, ny, n // ny),
        mesh=mesh,
        in_specs=(
            P(("dp", "expert"), "tensor"),
            P(("dp", "expert")),
            P(("dp", "expert"), "tensor"),
            P(("dp", "expert"), None),
            P(("dp", "expert"), None),
            P(("dp", "expert"), "tensor", None),
            P(("dp", "expert"), "tensor", None),
            P(("dp", "expert"), "tensor", None),
        ),
        out_specs=(P(("dp", "expert"), "tensor"), P(("dp", "expert"), None)),
        check_vma=False,
    )
```

```python
import functools

import jax
import jax.numpy as jnp
from jax import lax
from jax.experimental import pallas as pl
from jax.experimental.pallas import tpu as pltpu
from jax.sharding import PartitionSpec as P

F32, BF16 = jnp.float32, jnp.bfloat16
NT = (((1,), (1,)), ((), ()))


def send_order(ny, nz):
    if (ny, nz) != (8, 8):
        return [(y, z) for y in range(ny) for z in range(nz)]

    def ring(u, v):
        images = []
        for y, z in ((u, v), (-u, -v), (v, -u), (-v, u)):
            if (y % ny, z % nz) not in images:
                images.append((y % ny, z % nz))
        return images

    return (
        (ring(0, 0) + ring(4, 4) + ring(0, 4) + ring(2, 2))
        + (ring(0, 1) + ring(3, 4))
        + (ring(0, 2) + ring(2, 4))
        + (ring(1, 1) + ring(3, 3))
        + (ring(0, 3) + ring(1, 4))
        + (ring(1, 2) + ring(2, 3))
        + (ring(1, -2) + ring(2, -3))
        + (ring(1, 3) + ring(1, -3))
    )


def kernel(
    ny,
    nz,
    ids,
    gates,
    scales,
    ck,
    og,
    wg,
    wu,
    wd,
    out,
    terms_out,
    raw,
    hot,
    mix_hi,
    mix_lo,
    sendb,
    rows,
    w,
    psend,
    pin,
    keep,
    other_part,
    term_part,
    pre,
    ret,
    came,
    term_half,
    term_in,
    term_ret,
    term_came,
    loc_sem,
    a_send,
    a_recv,
    w_send,
    w_recv,
    d_send,
    d_recv,
    b_send,
    b_recv,
    p_send,
    p_recv,
    r_send,
    r_recv,
    s_send,
    s_recv,
    t_send,
    t_recv,
    ready,
):
    order = send_order(ny, nz)
    peers = ny * nz
    groups = keep.shape[0]
    per = peers // groups
    cap, part = sendb.shape[3:]
    half = 2 * part
    picks, tokens = ids.shape
    dp = lax.axis_index("dp")
    x = lax.axis_index("tensor")
    chip = lax.axis_index("expert")
    yy, zz = chip // nz, chip % nz
    h = x // 2
    a = (x + x // 2) % 2
    me = x % 2
    mate = 1 - me
    core = (dp + a) % 2
    a_peer = {"tensor": 2 * h + mate}
    b_peer = {"tensor": 3 - x}
    cross_peer = {"tensor": 2 * h + mate, "dp": 1 - dp}
    to_y = [((yy + d) % ny) * nz for d in range(ny)]
    to_z = [(zz + d) % nz for d in range(nz)]

    def target(n):
        y, z = order[n]
        return {"dp": core, "expert": to_y[y] + to_z[z]}

    def origin(n, plane):
        y, z = order[n]
        return {"dp": core, "tensor": plane, "expert": to_y[-y % ny] + to_z[-z % nz]}

    def each(first, count, act):
        for n in range(first, first + count):
            if n == 0:
                pl.when(a == 1)(functools.partial(act, n))
            else:
                act(n)

    def remote(src, dst, send, recv, where):
        return pltpu.make_async_remote_copy(
            src_ref=src, dst_ref=dst, send_sem=send, recv_sem=recv, device_id=where
        )

    def one_wait(g, ref, wait):
        @pl.when((a == 1) | (g > 0))
        def _():
            wait(ref.at[pl.ds(g * per, per)])

        if per > 1:

            @pl.when((a == 0) & (g == 0))
            def _():
                wait(ref.at[pl.ds(1, per - 1)])

    weights = (wg, wu, wd)
    local = [
        pltpu.make_async_copy(ck, raw.at[me, 0], loc_sem.at[0]),
        pltpu.make_async_copy(og, raw.at[me, 1], loc_sem.at[1]),
    ]
    for m in range(3):
        for f in range(2):
            local.append(
                pltpu.make_async_copy(
                    weights[m].at[:, pl.ds(f * half, half)], w.at[m, me, f], loc_sem.at[2 + 2 * m + f]
                )
            )
    for copy in local:
        copy.start()

    barrier = pltpu.get_barrier_semaphore()
    for step in range(1, 4):
        pl.semaphore_signal(barrier, inc=1, device_id={"tensor": (x + step) % 4})
    pl.semaphore_signal(barrier, inc=1, device_id=cross_peer)
    each(0, peers, lambda n: pl.semaphore_signal(barrier, inc=1, device_id=target(n)))

    r = lax.broadcasted_iota(jnp.int32, (peers, tokens), 0)
    expert = jnp.zeros((peers, tokens), jnp.int32)
    for n in range(peers):
        y, z = order[n]
        expert = jnp.where(r == n, core * peers + to_y[y] + to_z[z], expert)
    before = lax.broadcasted_iota(jnp.int32, (tokens, tokens), 0) < lax.broadcasted_iota(
        jnp.int32, (tokens, tokens), 1
    )
    before = before.astype(F32).astype(BF16)
    slot = lax.broadcasted_iota(jnp.int32, (peers, cap, tokens), 1).astype(F32)
    experts = (expert, expert + (1 - 2 * core) * peers)

    def choose(side):
        member = jnp.zeros((peers, tokens), F32)
        gate = jnp.zeros((peers, tokens), F32)
        for k in range(picks):
            same = ids[pl.ds(k, 1), :] == experts[side]
            member = jnp.where(same, 1.0, member)
            gate = jnp.where(same, gates[pl.ds(k, 1), :], gate)
        place = jnp.dot(member.astype(BF16), before, preferred_element_type=F32)
        place = jnp.where(member > 0.0, place, -1.0)
        pick = jnp.where(place[:, None, :] == slot, 1.0, 0.0)
        hot[side] = pick.reshape(groups, per * cap, tokens).astype(BF16)
        mix = (pick * gate[:, None, :]).reshape(peers * cap, tokens).T
        high = mix.astype(BF16)
        mix_hi[side] = high
        mix_lo[side] = (mix - high.astype(F32)).astype(BF16)

    choose(0)
    diagonal = lax.broadcasted_iota(jnp.int32, (tokens, tokens), 0) == lax.broadcasted_iota(
        jnp.int32, (tokens, tokens), 1
    )
    scale = jnp.sum(jnp.where(diagonal, scales[...], 0.0), axis=1, keepdims=True)

    def build(q):
        sources = ((raw[q, 0].astype(F32) * scale).astype(BF16), raw[q, 1])

        def group(g, carry):
            chosen = hot[0, g]
            for i in range(2):
                got = jnp.dot(chosen, sources[i], preferred_element_type=F32)
                sendb[q, pl.ds(g * per, per), i] = got.reshape(per, cap, part).astype(BF16)
            return carry

        lax.fori_loop(0, groups, group, 0)

        @pl.when(a == 0)
        def _():
            rows[2 * h + q, 0] = sendb[q, 0]

    def dispatch(q, turn):
        each(
            0,
            peers,
            lambda n: remote(
                sendb.at[q, n],
                rows.at[2 * h + q, n],
                d_send.at[turn, n // per],
                d_recv.at[turn, n // per],
                target(n),
            ).start(),
        )

    def forward(q, turn, g):
        one_wait(
            g,
            rows.at[2 * h + q],
            lambda ref: remote(ref, ref, d_send.at[turn, g], d_recv.at[turn, g], b_peer).wait_recv(),
        )
        ref = rows.at[2 * h + q, pl.ds(g * per, per)]
        remote(ref, ref, b_send.at[turn, g], b_recv.at[turn, g], b_peer).start()

    for i in range(2):
        local[i].wait()
    build(me)
    pl.semaphore_wait(barrier, peers + 3 + a)
    pl.semaphore_signal(ready, inc=1, device_id=cross_peer)

    a_copies = [
        remote(ck, raw.at[me, 0], a_send.at[0], a_recv.at[0], a_peer),
        remote(og, raw.at[me, 1], a_send.at[1], a_recv.at[1], a_peer),
    ]
    for m in range(3):
        for f in range(2):
            a_copies.append(
                remote(
                    weights[m].at[:, pl.ds(f * half, half)],
                    w.at[m, me, f],
                    w_send.at[2 * m + f],
                    w_recv.at[2 * m + f],
                    a_peer,
                )
            )
    for copy in a_copies:
        copy.start()
    dispatch(me, 0)
    choose(1)
    for i in range(2):
        remote(ck, raw.at[mate, i], a_send.at[i], a_recv.at[i], a_peer).wait_recv()
    build(mate)
    dispatch(mate, 1)
    small = max(1, groups // 4)

    def product(first, count, i, m, q):
        total = 0.0
        for fq in range(4):
            lanes = slice((fq % 2) * part, (fq % 2 + 1) * part)
            value = rows[fq, pl.ds(first * per, count * per), i].astype(F32)
            value = value.reshape(count * per * cap, part).astype(BF16)
            total += lax.dot_general(
                value, w[m, q, fq // 2, :, lanes], NT, preferred_element_type=F32
            )
        return total

    def grads(gate_pre, up_pre, back):
        sigma = jax.nn.sigmoid(gate_pre)
        swish = gate_pre * sigma
        hidden = (swish * up_pre).astype(BF16)
        term = jnp.sum(hidden.astype(F32) * back, axis=1, keepdims=True)
        d_gate = (back * up_pre * sigma * (1.0 + gate_pre * (1.0 - sigma))).astype(BF16)
        d_up = (back * swish).astype(BF16)
        return term, d_gate, d_up

    def results(d_gate, d_up, q, f, count):
        result = jnp.dot(d_gate, w[0, q, f], preferred_element_type=F32)
        result = result + jnp.dot(d_up, w[1, q, f], preferred_element_type=F32)
        return result.reshape(count, per * cap, half)

    def weight_landed(m):
        for f in range(2):
            remote(
                w.at[m, mate, f], w.at[m, mate, f], w_send.at[2 * m + f], w_recv.at[2 * m + f], a_peer
            ).wait_recv()

    def early(first, count, m):
        value = product(first, count, 0, m, mate)
        pre[m, pl.ds(first, count)] = value.reshape(count, per * cap, value.shape[-1])

    def own_quarter(c):
        first = c * small
        for i in range(small):
            other = rows.at[0, pl.ds((first + i) * per, per)]
            for turn in range(2):
                remote(
                    other, other, b_send.at[turn, first + i], b_recv.at[turn, first + i], b_peer
                ).wait_recv()
        term, d_gate, d_up = grads(
            product(first, small, 0, 0, me), product(first, small, 0, 1, me), product(first, small, 1, 2, me)
        )
        where = pl.ds(first, small)
        other_part[where] = results(d_gate, d_up, me, 1 - h, small)
        keep[where] = results(d_gate, d_up, me, h, small)
        n_rows = small * per * cap
        term_part[where] = jnp.broadcast_to(term, (n_rows, 128)).reshape(small, per * cap, 128)
        early(first, small, 0)

    def forward_own(g, carry):
        forward(me, 0, g)
        return carry

    lax.fori_loop(0, groups, forward_own, 0)
    for i in range(2, 8):
        local[i].wait()
    weight_landed(0)
    steps = groups // small

    def forward_mate(c, carry):
        @pl.when(c < steps)
        def _():
            for i in range(small):
                forward(mate, 1, c * small + i)

        @pl.when(c == steps)
        def _():
            weight_landed(1)
            for k in range(steps - 1):
                early(k * small, small, 1)

        @pl.when(c > 0)
        def _():
            own_quarter(c - 1)

        return carry

    lax.fori_loop(0, steps + 1, forward_mate, 0)
    early((steps - 1) * small, small, 1)
    weight_landed(2)

    def give_back(g):
        remote(psend.at[g], pin.at[g], p_send.at[g], p_recv.at[g], b_peer).wait_recv()
        remote(term_half.at[g], term_in.at[g], t_send.at[g], t_recv.at[g], b_peer).wait_recv()
        total = (keep[g] + pin[g].astype(F32)).reshape(per, cap, half).astype(BF16)
        where = pl.ds(g * per, per)
        for q in range(2):
            ret[q, where] = total[:, :, q * part : (q + 1) * part]
        term_ret[where] = (term_half[g] + term_in[g])[:, None, :]

        def send(side, n):
            q, plane = ((me, x), (mate, 2 * h + mate))[side]
            to = origin(n, plane)
            remote(ret.at[q, n], came.at[side, n], r_send.at[side, g], r_recv.at[side, g], to).start()
            remote(
                term_ret.at[n], term_came.at[side, n], s_send.at[side, g], s_recv.at[side, g], to
            ).start()

        for n in range(g * per, g * per + per):
            send(1, n)
            each(n, 1, functools.partial(send, 0))

    def mate_quarter(c, carry):
        first = c * small
        where = pl.ds(first, small)
        n_rows = small * per * cap
        term, d_gate, d_up = grads(
            pre[0, where].reshape(n_rows, -1),
            pre[1, where].reshape(n_rows, -1),
            product(first, small, 1, 2, mate),
        )
        psend[where] = (other_part[where] + results(d_gate, d_up, mate, 1 - h, small)).astype(BF16)
        for i in range(small):
            g = first + i
            remote(psend.at[g], pin.at[g], p_send.at[g], p_recv.at[g], b_peer).start()
        keep[where] = keep[where] + results(d_gate, d_up, mate, h, small)
        term = term_part[where].reshape(n_rows, 128) + term
        lane = lax.broadcasted_iota(jnp.int32, (small * per, cap, 128), 2)
        at = lax.broadcasted_iota(jnp.int32, (small * per, cap, 128), 1)
        line = jnp.sum(jnp.where(lane == at, term.reshape(small * per, cap, 128), 0.0), axis=1)
        term_half[where] = line.reshape(small, per, 128)
        for i in range(small):
            g = first + i
            remote(term_half.at[g], term_in.at[g], t_send.at[g], t_recv.at[g], b_peer).start()
        return carry

    lax.fori_loop(0, steps, mate_quarter, 0)
    pl.semaphore_wait(ready, 1)
    for g in range(groups):
        give_back(g)

    @pl.when(a == 0)
    def _():
        came[0, 0] = ret[me, 0]
        term_came[0, 0] = term_ret[0]

    def returned(g, ref, side, sends, recvs):
        act = lambda ref: remote(ref, ref, sends.at[side, g], recvs.at[side, g], b_peer).wait_recv()
        if side == 0:
            one_wait(g, ref.at[0], act)
        else:
            act(ref.at[1, pl.ds(g * per, per)])

    def landed(g, carry):
        for side in range(2):
            returned(g, came, side, r_send, r_recv)
            returned(g, term_came, side, s_send, s_recv)
        return carry

    lax.fori_loop(0, groups, landed, 0)
    mixed = 0.0
    for side in range(2):
        back_rows = came[side].astype(F32).reshape(peers * cap, part).astype(BF16)
        mixed += jnp.dot(mix_hi[side], back_rows, preferred_element_type=F32)
        mixed += jnp.dot(mix_lo[side], back_rows, preferred_element_type=F32)
    out[...] = mixed.astype(BF16)

    lane = lax.broadcasted_iota(jnp.int32, (peers, cap, 128), 2)
    at = lax.broadcasted_iota(jnp.int32, (peers, cap, 128), 1)
    by_expert = []
    for side in range(2):
        line = term_came[side].reshape(peers, 128)
        seen = jnp.sum(jnp.where(lane == at, line[:, None, :], 0.0), axis=2, keepdims=True)
        chosen = hot[side].astype(F32).reshape(peers, cap, tokens)
        by_expert.append(jnp.sum(chosen * seen, axis=1))
    for k in range(picks):
        total = 0.0
        for side in range(2):
            same = ids[pl.ds(k, 1), :] == experts[side]
            total += jnp.sum(jnp.where(same, by_expert[side], 0.0), axis=0, keepdims=True)
        terms_out[pl.ds(k, 1), :] = total

    for copy in a_copies:
        copy.wait_send()

    def drain(g, carry):
        for turn, q in enumerate((me, mate)):
            one_wait(
                g,
                sendb.at[q],
                lambda ref: remote(ref, ref, d_send.at[turn, g], d_recv.at[turn, g], b_peer).wait_send(),
            )
            ref = rows.at[2 * h + q, pl.ds(g * per, per)]
            remote(ref, ref, b_send.at[turn, g], b_recv.at[turn, g], b_peer).wait_send()
        for side, q in enumerate((me, mate)):
            if side == 0:
                one_wait(
                    g,
                    ret.at[q],
                    lambda ref: remote(ref, ref, r_send.at[0, g], r_recv.at[0, g], b_peer).wait_send(),
                )
                one_wait(
                    g,
                    term_ret,
                    lambda ref: remote(ref, ref, s_send.at[0, g], s_recv.at[0, g], b_peer).wait_send(),
                )
            else:
                for ref, sends, recvs in ((ret.at[q], r_send, r_recv), (term_ret, s_send, s_recv)):
                    ref = ref.at[pl.ds(g * per, per)]
                    remote(ref, ref, sends.at[1, g], recvs.at[1, g], b_peer).wait_send()
        remote(term_half.at[g], term_in.at[g], t_send.at[g], t_recv.at[g], b_peer).wait_send()
        remote(psend.at[g], pin.at[g], p_send.at[g], p_recv.at[g], b_peer).wait_send()
        return carry

    lax.fori_loop(0, groups, drain, 0)


def body(ny, nz, checkpoint, scales, out_grad, expert_ids, gates, w_gate, w_up, w_down):
    tokens, part = checkpoint.shape
    picks = expert_ids.shape[1]
    peers = ny * nz
    cap = tokens * picks // (2 * peers)
    hidden = w_gate.shape[1]
    half = 2 * part
    groups = max(2, peers // 8)
    group_rows = peers * cap // groups
    dma = pltpu.SemaphoreType.DMA
    vmem = pl.BlockSpec(memory_space=pltpu.VMEM)
    anyw = pl.BlockSpec(memory_space=pl.ANY)
    out, terms = pl.pallas_call(
        functools.partial(kernel, ny, nz),
        name="experts",
        out_shape=(
            jax.ShapeDtypeStruct((tokens, part), BF16),
            jax.ShapeDtypeStruct((picks, tokens), F32),
        ),
        in_specs=[vmem, vmem, vmem] + [anyw] * 5,
        out_specs=(vmem, vmem),
        scratch_shapes=[
            pltpu.VMEM((2, 2, tokens, part), BF16),
            pltpu.VMEM((2, groups, group_rows, tokens), BF16),
            pltpu.VMEM((2, tokens, peers * cap), BF16),
            pltpu.VMEM((2, tokens, peers * cap), BF16),
            pltpu.VMEM((2, peers, 2, cap, part), BF16),
            pltpu.VMEM((4, peers, 2, cap, part), BF16),
            pltpu.VMEM((3, 2, 2, hidden, half), BF16),
            pltpu.VMEM((groups, group_rows, half), BF16),
            pltpu.VMEM((groups, group_rows, half), BF16),
            pltpu.VMEM((groups, group_rows, half), F32),
            pltpu.VMEM((groups, group_rows, half), F32),
            pltpu.VMEM((groups, group_rows, 128), F32),
            pltpu.VMEM((2, groups, group_rows, hidden), F32),
            pltpu.VMEM((2, peers, cap, part), BF16),
            pltpu.VMEM((2, peers, cap, part), BF16),
            pltpu.VMEM((groups, peers // groups, 128), F32),
            pltpu.VMEM((groups, peers // groups, 128), F32),
            pltpu.VMEM((peers, 1, 128), F32),
            pltpu.VMEM((2, peers, 1, 128), F32),
            dma((8,)),
            dma((2,)),
            dma((2,)),
            dma((6,)),
            dma((6,)),
            dma((2, groups)),
            dma((2, groups)),
            dma((2, groups)),
            dma((2, groups)),
            dma((groups,)),
            dma((groups,)),
            dma((2, groups)),
            dma((2, groups)),
            dma((2, groups)),
            dma((2, groups)),
            dma((groups,)),
            dma((groups,)),
            pltpu.SemaphoreType.REGULAR,
        ],
        compiler_params=pltpu.CompilerParams(
            collective_id=0, has_side_effects=True, vmem_limit_bytes=60 * 1024 * 1024
        ),
    )(
        expert_ids.T,
        gates.T,
        scales[None, :],
        checkpoint,
        out_grad,
        w_gate[0],
        w_up[0],
        w_down[0],
    )
    return out, terms.T


def solution(mesh):
    n = mesh.shape["expert"]
    ny = 8 if n == 64 else n
    return jax.shard_map(
        functools.partial(body, ny, n // ny),
        mesh=mesh,
        in_specs=(
            P(("dp", "expert"), "tensor"),
            P(("dp", "expert")),
            P(("dp", "expert"), "tensor"),
            P(("dp", "expert"), None),
            P(("dp", "expert"), None),
            P(("dp", "expert"), "tensor", None),
            P(("dp", "expert"), "tensor", None),
            P(("dp", "expert"), "tensor", None),
        ),
        out_specs=(P(("dp", "expert"), "tensor"), P(("dp", "expert"), None)),
        check_vma=False,
    )
```

```python
import functools

import jax
import jax.numpy as jnp
from jax import lax
from jax.experimental import pallas as pl
from jax.experimental.pallas import tpu as pltpu
from jax.sharding import PartitionSpec as P

F32, BF16 = jnp.float32, jnp.bfloat16
NT = (((1,), (1,)), ((), ()))


def send_order(ny, nz):
    if (ny, nz) != (8, 8):
        return [(y, z) for y in range(ny) for z in range(nz)]

    def ring(u, v):
        images = []
        for y, z in ((u, v), (-u, -v), (v, -u), (-v, u)):
            if (y % ny, z % nz) not in images:
                images.append((y % ny, z % nz))
        return images

    return (
        (ring(0, 0) + ring(4, 4) + ring(0, 4) + ring(2, 2))
        + (ring(0, 1) + ring(3, 4))
        + (ring(0, 2) + ring(2, 4))
        + (ring(1, 1) + ring(3, 3))
        + (ring(0, 3) + ring(1, 4))
        + (ring(1, 2) + ring(2, 3))
        + (ring(1, -2) + ring(2, -3))
        + (ring(1, 3) + ring(1, -3))
    )


def kernel(
    ny,
    nz,
    ids,
    gates,
    scales,
    ck,
    og,
    wg,
    wu,
    wd,
    out,
    terms_out,
    raw,
    hot,
    mix_hi,
    mix_lo,
    sendb,
    rows,
    w,
    psend,
    pin,
    keep,
    other_part,
    term_part,
    pre,
    ret,
    came,
    term_half,
    term_in,
    term_ret,
    term_came,
    loc_sem,
    a_send,
    a_recv,
    w_send,
    w_recv,
    d_send,
    d_recv,
    b_send,
    b_recv,
    p_send,
    p_recv,
    r_send,
    r_recv,
    s_send,
    s_recv,
    t_send,
    t_recv,
    c_send,
    c_recv,
    k_send,
    k_recv,
    ready,
):
    order = send_order(ny, nz)
    peers = ny * nz
    groups = keep.shape[1]
    per = peers // groups
    cap, part = sendb.shape[3:]
    half = 2 * part
    picks, tokens = ids.shape
    dp = lax.axis_index("dp")
    x = lax.axis_index("tensor")
    chip = lax.axis_index("expert")
    yy, zz = chip // nz, chip % nz
    h = x // 2
    a = (x + x // 2) % 2
    me = x % 2
    mate = 1 - me
    core = (dp + a) % 2
    a_peer = {"tensor": 2 * h + mate}
    b_peer = {"tensor": 3 - x, "dp": core}
    sibling = {"dp": 1 - dp}
    to_y = [((yy + d) % ny) * nz for d in range(ny)]
    to_z = [(zz + d) % nz for d in range(nz)]

    def target(n):
        y, z = order[n]
        return {"expert": to_y[y] + to_z[z]}

    def origin(n, plane):
        y, z = order[n]
        return {"tensor": plane, "expert": to_y[-y % ny] + to_z[-z % nz]}

    def landing(q):
        return (1 - a) * (2 * h + q) + a * (4 + q)

    def each(first, count, act):
        for n in range(max(first, 1), first + count):
            act(n)

    def remote(src, dst, send, recv, where):
        return pltpu.make_async_remote_copy(
            src_ref=src, dst_ref=dst, send_sem=send, recv_sem=recv, device_id=where
        )

    def one_wait(g, ref, wait):
        @pl.when(g > 0)
        def _():
            wait(ref.at[pl.ds(g * per, per)])

        if per > 1:

            @pl.when(g == 0)
            def _():
                wait(ref.at[pl.ds(1, per - 1)])

    weights = (wg, wu, wd)
    local = [
        pltpu.make_async_copy(ck, raw.at[me, 0], loc_sem.at[0]),
        pltpu.make_async_copy(og, raw.at[me, 1], loc_sem.at[1]),
    ]
    for m in range(3):
        for f in range(2):
            local.append(
                pltpu.make_async_copy(
                    weights[m].at[:, pl.ds(f * half, half)], w.at[m, me, f], loc_sem.at[2 + 2 * m + f]
                )
            )
    for copy in local:
        copy.start()

    barrier = pltpu.get_barrier_semaphore()
    for step in range(1, 4):
        pl.semaphore_signal(barrier, inc=1, device_id={"tensor": (x + step) % 4})
    pl.semaphore_signal(barrier, inc=1, device_id=sibling)
    pl.semaphore_signal(barrier, inc=1, device_id={"tensor": 3 - x, "dp": 1 - dp})
    each(0, peers, lambda n: pl.semaphore_signal(barrier, inc=1, device_id=target(n)))

    r = lax.broadcasted_iota(jnp.int32, (peers, tokens), 0)
    expert = jnp.zeros((peers, tokens), jnp.int32)
    for n in range(peers):
        y, z = order[n]
        expert = jnp.where(r == n, core * peers + to_y[y] + to_z[z], expert)
    before = lax.broadcasted_iota(jnp.int32, (tokens, tokens), 0) < lax.broadcasted_iota(
        jnp.int32, (tokens, tokens), 1
    )
    before = before.astype(F32).astype(BF16)
    slot = lax.broadcasted_iota(jnp.int32, (peers, cap, tokens), 1).astype(F32)
    experts = (expert, expert + (1 - 2 * core) * peers)

    def choose(side):
        member = jnp.zeros((peers, tokens), F32)
        gate = jnp.zeros((peers, tokens), F32)
        for k in range(picks):
            same = ids[pl.ds(k, 1), :] == experts[side]
            member = jnp.where(same, 1.0, member)
            gate = jnp.where(same, gates[pl.ds(k, 1), :], gate)
        place = jnp.dot(member.astype(BF16), before, preferred_element_type=F32)
        place = jnp.where(member > 0.0, place, -1.0)
        pick = jnp.where(place[:, None, :] == slot, 1.0, 0.0)
        hot[side] = pick.reshape(groups, per * cap, tokens).astype(BF16)
        mix = (pick * gate[:, None, :]).reshape(peers * cap, tokens).T
        high = mix.astype(BF16)
        mix_hi[side] = high
        mix_lo[side] = (mix - high.astype(F32)).astype(BF16)

    choose(0)
    diagonal = lax.broadcasted_iota(jnp.int32, (tokens, tokens), 0) == lax.broadcasted_iota(
        jnp.int32, (tokens, tokens), 1
    )
    scale = jnp.sum(jnp.where(diagonal, scales[...], 0.0), axis=1, keepdims=True)

    def build(q):
        sources = ((raw[q, 0].astype(F32) * scale).astype(BF16), raw[q, 1])

        def group(g, carry):
            chosen = hot[0, g]
            for i in range(2):
                got = jnp.dot(chosen, sources[i], preferred_element_type=F32)
                sendb[q, pl.ds(g * per, per), i] = got.reshape(per, cap, part).astype(BF16)
            return carry

        lax.fori_loop(0, groups, group, 0)

        rows[landing(q), 0] = sendb[q, 0]

    def dispatch(q, turn):
        each(
            0,
            peers,
            lambda n: remote(
                sendb.at[q, n],
                rows.at[landing(q), n],
                d_send.at[turn, n // per],
                d_recv.at[turn, n // per],
                target(n),
            ).start(),
        )

    def forward(q, turn, g):
        one_wait(
            g,
            rows.at[landing(q)],
            lambda ref: remote(ref, ref, d_send.at[turn, g], d_recv.at[turn, g], b_peer).wait_recv(),
        )
        ref = rows.at[landing(q), pl.ds(g * per, per)]
        place = rows.at[2 * h + q, pl.ds(g * per, per)]
        remote(ref, place, b_send.at[turn, g], b_recv.at[turn, g], b_peer).start()

        @pl.when(a == 1)
        def _():
            remote(ref, place, c_send.at[turn, g], c_recv.at[turn, g], sibling).start()

    for i in range(2):
        local[i].wait()
    build(me)
    pl.semaphore_wait(barrier, peers + 4)
    pl.semaphore_signal(ready, inc=1, device_id=a_peer)

    a_copies = [
        remote(ck, raw.at[me, 0], a_send.at[0], a_recv.at[0], a_peer),
        remote(og, raw.at[me, 1], a_send.at[1], a_recv.at[1], a_peer),
    ]
    for m in range(3):
        for f in range(2):
            a_copies.append(
                remote(
                    weights[m].at[:, pl.ds(f * half, half)],
                    w.at[m, me, f],
                    w_send.at[2 * m + f],
                    w_recv.at[2 * m + f],
                    a_peer,
                )
            )
    for copy in a_copies:
        copy.start()
    dispatch(me, 0)
    choose(1)
    for i in range(2):
        remote(ck, raw.at[mate, i], a_send.at[i], a_recv.at[i], a_peer).wait_recv()
    build(mate)
    dispatch(mate, 1)
    small = max(1, groups // 4)

    def product(first, count, i, m, q):
        total = 0.0
        for fq in range(4):
            lanes = slice((fq % 2) * part, (fq % 2 + 1) * part)
            value = rows[fq, pl.ds(first * per, count * per), i].astype(F32)
            value = value.reshape(count * per * cap, part).astype(BF16)
            total += lax.dot_general(
                value, w[m, q, fq // 2, :, lanes], NT, preferred_element_type=F32
            )
        return total

    def grads(gate_pre, up_pre, back):
        sigma = jax.nn.sigmoid(gate_pre)
        swish = gate_pre * sigma
        hidden = (swish * up_pre).astype(BF16)
        term = jnp.sum(hidden.astype(F32) * back, axis=1, keepdims=True)
        d_gate = (back * up_pre * sigma * (1.0 + gate_pre * (1.0 - sigma))).astype(BF16)
        d_up = (back * swish).astype(BF16)
        return term, d_gate, d_up

    def results(d_gate, d_up, q, f, count):
        result = jnp.dot(d_gate, w[0, q, f], preferred_element_type=F32)
        result = result + jnp.dot(d_up, w[1, q, f], preferred_element_type=F32)
        return result.reshape(count, per * cap, half)

    def weight_landed(m):
        for f in range(2):
            remote(
                w.at[m, mate, f], w.at[m, mate, f], w_send.at[2 * m + f], w_recv.at[2 * m + f], a_peer
            ).wait_recv()

    def early(first, count, m):
        value = product(first, count, 0, m, mate)
        pre[m, pl.ds(first, count)] = value.reshape(count, per * cap, value.shape[-1])

    def own_quarter(c):
        first = c * small
        for i in range(small):
            other = rows.at[0, pl.ds((first + i) * per, per)]
            for turn in range(2):
                g = first + i
                remote(other, other, b_send.at[turn, g], b_recv.at[turn, g], b_peer).wait_recv()

                @pl.when(a == 1)
                def _():
                    remote(other, other, c_send.at[turn, g], c_recv.at[turn, g], sibling).wait_recv()
        term, d_gate, d_up = grads(
            product(first, small, 0, 0, me), product(first, small, 0, 1, me), product(first, small, 1, 2, me)
        )
        where = pl.ds(first, small)
        other_part[where] = results(d_gate, d_up, me, 1 - h, small)
        keep[0, where] = results(d_gate, d_up, me, h, small)
        n_rows = small * per * cap
        term_part[where] = jnp.broadcast_to(term, (n_rows, 128)).reshape(small, per * cap, 128)
        early(first, small, 0)

    def forward_own(g, carry):
        forward(me, 0, g)
        return carry

    lax.fori_loop(0, groups, forward_own, 0)
    for i in range(2, 8):
        local[i].wait()
    weight_landed(0)
    steps = groups // small

    def forward_mate(c, carry):
        @pl.when(c < steps)
        def _():
            for i in range(small):
                forward(mate, 1, c * small + i)

        @pl.when(c == steps)
        def _():
            weight_landed(1)
            for k in range(steps - 1):
                early(k * small, small, 1)

        @pl.when(c > 0)
        def _():
            own_quarter(c - 1)

        return carry

    lax.fori_loop(0, steps + 1, forward_mate, 0)
    early((steps - 1) * small, small, 1)
    weight_landed(2)

    def to_sibling(g):
        return (
            remote(keep.at[0, g], keep.at[1, g], k_send.at[0, g], k_recv.at[0, g], sibling),
            remote(term_half.at[0, g], term_half.at[1, g], k_send.at[1, g], k_recv.at[1, g], sibling),
        )

    def give_back(g):
        @pl.when(a == 1)
        def _():
            for copy in to_sibling(g):
                copy.wait_recv()

        remote(psend.at[g], pin.at[g], p_send.at[g], p_recv.at[g], b_peer).wait_recv()
        remote(term_half.at[0, g], term_in.at[g], t_send.at[g], t_recv.at[g], b_peer).wait_recv()
        total = (keep[a, g] + pin[g].astype(F32)).reshape(per, cap, half).astype(BF16)
        where = pl.ds(g * per, per)
        for q in range(2):
            ret[q, where] = total[:, :, q * part : (q + 1) * part]
        term_ret[where] = (term_half[a, g] + term_in[g])[:, None, :]

        def send(side, n):
            q, plane = ((me, x), (mate, 2 * h + mate))[side]
            to = origin(n, plane)
            remote(ret.at[q, n], came.at[side, n], r_send.at[side, g], r_recv.at[side, g], to).start()
            remote(
                term_ret.at[n], term_came.at[side, n], s_send.at[side, g], s_recv.at[side, g], to
            ).start()

        for n in range(g * per, g * per + per):
            send(1, n)
            each(n, 1, functools.partial(send, 0))

    def mate_quarter(c, carry):
        first = c * small
        where = pl.ds(first, small)
        n_rows = small * per * cap
        term, d_gate, d_up = grads(
            pre[0, where].reshape(n_rows, -1),
            pre[1, where].reshape(n_rows, -1),
            product(first, small, 1, 2, mate),
        )
        psend[where] = (other_part[where] + results(d_gate, d_up, mate, 1 - h, small)).astype(BF16)
        for i in range(small):
            g = first + i
            remote(psend.at[g], pin.at[g], p_send.at[g], p_recv.at[g], b_peer).start()
        keep[0, where] = keep[0, where] + results(d_gate, d_up, mate, h, small)
        term = term_part[where].reshape(n_rows, 128) + term
        lane = lax.broadcasted_iota(jnp.int32, (small * per, cap, 128), 2)
        at = lax.broadcasted_iota(jnp.int32, (small * per, cap, 128), 1)
        line = jnp.sum(jnp.where(lane == at, term.reshape(small * per, cap, 128), 0.0), axis=1)
        term_half[0, where] = line.reshape(small, per, 128)
        for i in range(small):
            g = first + i
            remote(term_half.at[0, g], term_in.at[g], t_send.at[g], t_recv.at[g], b_peer).start()

            @pl.when(a == 1)
            def _():
                for copy in to_sibling(g):
                    copy.start()
        return carry

    lax.fori_loop(0, steps, mate_quarter, 0)
    pl.semaphore_wait(ready, 1)
    for g in range(groups):
        give_back(g)

    came[0, 0] = ret[me, 0]
    term_came[0, 0] = term_ret[0]

    def returned(g, ref, side, sends, recvs):
        act = lambda ref: remote(ref, ref, sends.at[side, g], recvs.at[side, g], b_peer).wait_recv()
        if side == 0:
            one_wait(g, ref.at[0], act)
        else:
            act(ref.at[1, pl.ds(g * per, per)])

    def landed(g, carry):
        for side in range(2):
            returned(g, came, side, r_send, r_recv)
            returned(g, term_came, side, s_send, s_recv)
        return carry

    lax.fori_loop(0, groups, landed, 0)
    mixed = 0.0
    for side in range(2):
        back_rows = came[side].astype(F32).reshape(peers * cap, part).astype(BF16)
        mixed += jnp.dot(mix_hi[side], back_rows, preferred_element_type=F32)
        mixed += jnp.dot(mix_lo[side], back_rows, preferred_element_type=F32)
    out[...] = mixed.astype(BF16)

    lane = lax.broadcasted_iota(jnp.int32, (peers, cap, 128), 2)
    at = lax.broadcasted_iota(jnp.int32, (peers, cap, 128), 1)
    by_expert = []
    for side in range(2):
        line = term_came[side].reshape(peers, 128)
        seen = jnp.sum(jnp.where(lane == at, line[:, None, :], 0.0), axis=2, keepdims=True)
        chosen = hot[side].astype(F32).reshape(peers, cap, tokens)
        by_expert.append(jnp.sum(chosen * seen, axis=1))
    for k in range(picks):
        total = 0.0
        for side in range(2):
            same = ids[pl.ds(k, 1), :] == experts[side]
            total += jnp.sum(jnp.where(same, by_expert[side], 0.0), axis=0, keepdims=True)
        terms_out[pl.ds(k, 1), :] = total

    for copy in a_copies:
        copy.wait_send()

    def drain(g, carry):
        for turn, q in enumerate((me, mate)):
            one_wait(
                g,
                sendb.at[q],
                lambda ref: remote(ref, ref, d_send.at[turn, g], d_recv.at[turn, g], b_peer).wait_send(),
            )
            ref = rows.at[landing(q), pl.ds(g * per, per)]
            remote(ref, ref, b_send.at[turn, g], b_recv.at[turn, g], b_peer).wait_send()

            @pl.when(a == 1)
            def _():
                remote(ref, ref, c_send.at[turn, g], c_recv.at[turn, g], sibling).wait_send()

        for side, q in enumerate((me, mate)):
            if side == 0:
                one_wait(
                    g,
                    ret.at[q],
                    lambda ref: remote(ref, ref, r_send.at[0, g], r_recv.at[0, g], b_peer).wait_send(),
                )
                one_wait(
                    g,
                    term_ret,
                    lambda ref: remote(ref, ref, s_send.at[0, g], s_recv.at[0, g], b_peer).wait_send(),
                )
            else:
                for ref, sends, recvs in ((ret.at[q], r_send, r_recv), (term_ret, s_send, s_recv)):
                    ref = ref.at[pl.ds(g * per, per)]
                    remote(ref, ref, sends.at[1, g], recvs.at[1, g], b_peer).wait_send()
        remote(term_half.at[0, g], term_in.at[g], t_send.at[g], t_recv.at[g], b_peer).wait_send()

        @pl.when(a == 1)
        def _():
            for copy in to_sibling(g):
                copy.wait_send()

        remote(psend.at[g], pin.at[g], p_send.at[g], p_recv.at[g], b_peer).wait_send()
        return carry

    lax.fori_loop(0, groups, drain, 0)


def body(ny, nz, checkpoint, scales, out_grad, expert_ids, gates, w_gate, w_up, w_down):
    tokens, part = checkpoint.shape
    picks = expert_ids.shape[1]
    peers = ny * nz
    cap = tokens * picks // (2 * peers)
    hidden = w_gate.shape[1]
    half = 2 * part
    groups = max(2, peers // 8)
    group_rows = peers * cap // groups
    dma = pltpu.SemaphoreType.DMA
    vmem = pl.BlockSpec(memory_space=pltpu.VMEM)
    anyw = pl.BlockSpec(memory_space=pl.ANY)
    out, terms = pl.pallas_call(
        functools.partial(kernel, ny, nz),
        name="experts",
        out_shape=(
            jax.ShapeDtypeStruct((tokens, part), BF16),
            jax.ShapeDtypeStruct((picks, tokens), F32),
        ),
        in_specs=[vmem, vmem, vmem] + [anyw] * 5,
        out_specs=(vmem, vmem),
        scratch_shapes=[
            pltpu.VMEM((2, 2, tokens, part), BF16),
            pltpu.VMEM((2, groups, group_rows, tokens), BF16),
            pltpu.VMEM((2, tokens, peers * cap), BF16),
            pltpu.VMEM((2, tokens, peers * cap), BF16),
            pltpu.VMEM((2, peers, 2, cap, part), BF16),
            pltpu.VMEM((6, peers, 2, cap, part), BF16),
            pltpu.VMEM((3, 2, 2, hidden, half), BF16),
            pltpu.VMEM((groups, group_rows, half), BF16),
            pltpu.VMEM((groups, group_rows, half), BF16),
            pltpu.VMEM((2, groups, group_rows, half), F32),
            pltpu.VMEM((groups, group_rows, half), F32),
            pltpu.VMEM((groups, group_rows, 128), F32),
            pltpu.VMEM((2, groups, group_rows, hidden), F32),
            pltpu.VMEM((2, peers, cap, part), BF16),
            pltpu.VMEM((2, peers, cap, part), BF16),
            pltpu.VMEM((2, groups, peers // groups, 128), F32),
            pltpu.VMEM((groups, peers // groups, 128), F32),
            pltpu.VMEM((peers, 1, 128), F32),
            pltpu.VMEM((2, peers, 1, 128), F32),
            dma((8,)),
            dma((2,)),
            dma((2,)),
            dma((6,)),
            dma((6,)),
            dma((2, groups)),
            dma((2, groups)),
            dma((2, groups)),
            dma((2, groups)),
            dma((groups,)),
            dma((groups,)),
            dma((2, groups)),
            dma((2, groups)),
            dma((2, groups)),
            dma((2, groups)),
            dma((groups,)),
            dma((groups,)),
            dma((2, groups)),
            dma((2, groups)),
            dma((2, groups)),
            dma((2, groups)),
            pltpu.SemaphoreType.REGULAR,
        ],
        compiler_params=pltpu.CompilerParams(
            collective_id=0, has_side_effects=True, vmem_limit_bytes=60 * 1024 * 1024
        ),
    )(
        expert_ids.T,
        gates.T,
        scales[None, :],
        checkpoint,
        out_grad,
        w_gate[0],
        w_up[0],
        w_down[0],
    )
    return out, terms.T


def solution(mesh):
    n = mesh.shape["expert"]
    ny = 8 if n == 64 else n
    return jax.shard_map(
        functools.partial(body, ny, n // ny),
        mesh=mesh,
        in_specs=(
            P(("dp", "expert"), "tensor"),
            P(("dp", "expert")),
            P(("dp", "expert"), "tensor"),
            P(("dp", "expert"), None),
            P(("dp", "expert"), None),
            P(("dp", "expert"), "tensor", None),
            P(("dp", "expert"), "tensor", None),
            P(("dp", "expert"), "tensor", None),
        ),
        out_specs=(P(("dp", "expert"), "tensor"), P(("dp", "expert"), None)),
        check_vma=False,
    )
```

```python
import functools

import jax
import jax.numpy as jnp
from jax import lax
from jax.experimental import pallas as pl
from jax.experimental.pallas import tpu as pltpu
from jax.sharding import PartitionSpec as P

F32, BF16 = jnp.float32, jnp.bfloat16
NT = (((1,), (1,)), ((), ()))


def send_order(ny, nz):
    if (ny, nz) != (8, 8):
        return [(y, z) for y in range(ny) for z in range(nz)]

    def ring(u, v):
        images = []
        for y, z in ((u, v), (-u, -v), (v, -u), (-v, u)):
            if (y % ny, z % nz) not in images:
                images.append((y % ny, z % nz))
        return images

    return (
        (ring(0, 0) + ring(4, 4) + ring(0, 4) + ring(2, 2))
        + (ring(0, 1) + ring(3, 4))
        + (ring(0, 2) + ring(2, 4))
        + (ring(1, 1) + ring(3, 3))
        + (ring(0, 3) + ring(1, 4))
        + (ring(1, 2) + ring(2, 3))
        + (ring(1, -2) + ring(2, -3))
        + (ring(1, 3) + ring(1, -3))
    )


def kernel(
    ny,
    nz,
    ids,
    gates,
    scales,
    ck,
    og,
    wg,
    wu,
    wd,
    out,
    terms_out,
    raw,
    hot,
    mix_hi,
    mix_lo,
    sendb,
    rows,
    w,
    psend,
    pin,
    keep,
    other_part,
    term_part,
    pre,
    ret,
    came,
    term_half,
    term_in,
    term_ret,
    term_came,
    part_t,
    part_in,
    loc_sem,
    a_send,
    a_recv,
    w_send,
    w_recv,
    d_send,
    d_recv,
    b_send,
    b_recv,
    p_send,
    p_recv,
    r_send,
    r_recv,
    s_send,
    s_recv,
    t_send,
    t_recv,
    c_send,
    c_recv,
    k_send,
    k_recv,
    x_send,
    x_recv,
    ready,
):
    order = send_order(ny, nz)
    peers = ny * nz
    groups = keep.shape[1]
    per = peers // groups
    cap, part = sendb.shape[3:]
    half = 2 * part
    picks, tokens = ids.shape
    dp = lax.axis_index("dp")
    x = lax.axis_index("tensor")
    chip = lax.axis_index("expert")
    yy, zz = chip // nz, chip % nz
    h = x // 2
    a = (x + x // 2) % 2
    me = x % 2
    mate = 1 - me
    core = (dp + a) % 2
    a_peer = {"tensor": 2 * h + mate}
    b_peer = {"tensor": 3 - x, "dp": core}
    sibling = {"dp": 1 - dp}
    to_y = [((yy + d) % ny) * nz for d in range(ny)]
    to_z = [(zz + d) % nz for d in range(nz)]

    def target(n):
        y, z = order[n]
        return {"expert": to_y[y] + to_z[z]}

    def origin(n, plane):
        y, z = order[n]
        return {"tensor": plane, "expert": to_y[-y % ny] + to_z[-z % nz]}

    def landing(q):
        return (1 - a) * (2 * h + q) + a * (4 + q)

    def each(first, count, act):
        for n in range(max(first, 1), first + count):
            act(n)

    def remote(src, dst, send, recv, where):
        return pltpu.make_async_remote_copy(
            src_ref=src, dst_ref=dst, send_sem=send, recv_sem=recv, device_id=where
        )

    def one_wait(g, ref, wait):
        @pl.when(g > 0)
        def _():
            wait(ref.at[pl.ds(g * per, per)])

        if per > 1:

            @pl.when(g == 0)
            def _():
                wait(ref.at[pl.ds(1, per - 1)])

    weights = (wg, wu, wd)
    local = [
        pltpu.make_async_copy(ck, raw.at[me, 0], loc_sem.at[0]),
        pltpu.make_async_copy(og, raw.at[me, 1], loc_sem.at[1]),
    ]
    for m in range(3):
        for f in range(2):
            local.append(
                pltpu.make_async_copy(
                    weights[m].at[:, pl.ds(f * half, half)], w.at[m, me, f], loc_sem.at[2 + 2 * m + f]
                )
            )
    for copy in local:
        copy.start()

    barrier = pltpu.get_barrier_semaphore()
    for step in range(1, 4):
        pl.semaphore_signal(barrier, inc=1, device_id={"tensor": (x + step) % 4})
    pl.semaphore_signal(barrier, inc=1, device_id=sibling)
    pl.semaphore_signal(barrier, inc=1, device_id={"tensor": 3 - x, "dp": 1 - dp})
    for n in sorted(range(1, peers), key=lambda n: -sum(min(d, m - d) for d, m in zip(order[n], (ny, nz)))):
        pl.semaphore_signal(barrier, inc=1, device_id=target(n))

    r = lax.broadcasted_iota(jnp.int32, (peers, tokens), 0)
    expert = jnp.zeros((peers, tokens), jnp.int32)
    for n in range(peers):
        y, z = order[n]
        expert = jnp.where(r == n, core * peers + to_y[y] + to_z[z], expert)
    before = lax.broadcasted_iota(jnp.int32, (tokens, tokens), 0) < lax.broadcasted_iota(
        jnp.int32, (tokens, tokens), 1
    )
    before = before.astype(F32).astype(BF16)
    slot = lax.broadcasted_iota(jnp.int32, (peers, cap, tokens), 1).astype(F32)
    experts = (expert, expert + (1 - 2 * core) * peers)

    def choose(side):
        member = jnp.zeros((peers, tokens), F32)
        gate = jnp.zeros((peers, tokens), F32)
        for k in range(picks):
            same = ids[pl.ds(k, 1), :] == experts[side]
            member = jnp.where(same, 1.0, member)
            gate = jnp.where(same, gates[pl.ds(k, 1), :], gate)
        place = jnp.dot(member.astype(BF16), before, preferred_element_type=F32)
        place = jnp.where(member > 0.0, place, -1.0)
        pick = jnp.where(place[:, None, :] == slot, 1.0, 0.0)
        hot[side] = pick.reshape(groups, per * cap, tokens).astype(BF16)
        mix = (pick * gate[:, None, :]).reshape(peers * cap, tokens).T
        high = mix.astype(BF16)
        mix_hi[side] = high
        mix_lo[side] = (mix - high.astype(F32)).astype(BF16)

    choose(0)
    diagonal = lax.broadcasted_iota(jnp.int32, (tokens, tokens), 0) == lax.broadcasted_iota(
        jnp.int32, (tokens, tokens), 1
    )
    scale = jnp.sum(jnp.where(diagonal, scales[...], 0.0), axis=1, keepdims=True)

    def build(q):
        sources = ((raw[q, 0].astype(F32) * scale).astype(BF16), raw[q, 1])

        def group(g, carry):
            chosen = hot[0, g]
            for i in range(2):
                got = jnp.dot(chosen, sources[i], preferred_element_type=F32)
                sendb[q, pl.ds(g * per, per), i] = got.reshape(per, cap, part).astype(BF16)
            return carry

        lax.fori_loop(0, groups, group, 0)

        rows[landing(q), 0] = sendb[q, 0]

    def dispatch(q, turn):
        each(
            0,
            peers,
            lambda n: remote(
                sendb.at[q, n],
                rows.at[landing(q), n],
                d_send.at[turn, n // per],
                d_recv.at[turn, n // per],
                target(n),
            ).start(),
        )

    def forward(q, turn, g):
        one_wait(
            g,
            rows.at[landing(q)],
            lambda ref: remote(ref, ref, d_send.at[turn, g], d_recv.at[turn, g], b_peer).wait_recv(),
        )
        ref = rows.at[landing(q), pl.ds(g * per, per)]
        place = rows.at[2 * h + q, pl.ds(g * per, per)]
        remote(ref, place, b_send.at[turn, g], b_recv.at[turn, g], b_peer).start()

        @pl.when(a == 1)
        def _():
            remote(ref, place, c_send.at[turn, g], c_recv.at[turn, g], sibling).start()

    for i in range(2):
        local[i].wait()
    build(me)
    pl.semaphore_wait(barrier, peers + 4)
    pl.semaphore_signal(ready, inc=1, device_id=a_peer)

    a_copies = [
        remote(ck, raw.at[me, 0], a_send.at[0], a_recv.at[0], a_peer),
        remote(og, raw.at[me, 1], a_send.at[1], a_recv.at[1], a_peer),
    ]
    for m in range(3):
        for f in range(2):
            a_copies.append(
                remote(
                    weights[m].at[:, pl.ds(f * half, half)],
                    w.at[m, me, f],
                    w_send.at[2 * m + f],
                    w_recv.at[2 * m + f],
                    a_peer,
                )
            )
    for copy in a_copies:
        copy.start()
    dispatch(me, 0)
    choose(1)
    ahead = min(3, groups - 1)

    def forward_own(g, carry):
        forward(me, 0, g)
        return carry

    lax.fori_loop(0, ahead, forward_own, 0)
    for i in range(2):
        remote(ck, raw.at[mate, i], a_send.at[i], a_recv.at[i], a_peer).wait_recv()
    build(mate)
    dispatch(mate, 1)
    small = max(1, groups // 4)

    def product(first, count, i, m, q):
        total = 0.0
        for fq in range(4):
            lanes = slice((fq % 2) * part, (fq % 2 + 1) * part)
            value = rows[fq, pl.ds(first * per, count * per), i].astype(F32)
            value = value.reshape(count * per * cap, part).astype(BF16)
            total += lax.dot_general(
                value, w[m, q, fq // 2, :, lanes], NT, preferred_element_type=F32
            )
        return total

    def grads(gate_pre, up_pre, back):
        sigma = jax.nn.sigmoid(gate_pre)
        swish = gate_pre * sigma
        hidden = (swish * up_pre).astype(BF16)
        term = jnp.sum(hidden.astype(F32) * back, axis=1, keepdims=True)
        d_gate = (back * up_pre * sigma * (1.0 + gate_pre * (1.0 - sigma))).astype(BF16)
        d_up = (back * swish).astype(BF16)
        return term, d_gate, d_up

    def results(d_gate, d_up, q, f, count):
        result = jnp.dot(d_gate, w[0, q, f], preferred_element_type=F32)
        result = result + jnp.dot(d_up, w[1, q, f], preferred_element_type=F32)
        return result.reshape(count, per * cap, half)

    def weight_landed(m):
        for f in range(2):
            remote(
                w.at[m, mate, f], w.at[m, mate, f], w_send.at[2 * m + f], w_recv.at[2 * m + f], a_peer
            ).wait_recv()

    def early(first, count, m):
        value = product(first, count, 0, m, mate)
        pre[m, pl.ds(first, count)] = value.reshape(count, per * cap, value.shape[-1])

    def own_quarter(c):
        first = c * small
        for i in range(small):
            other = rows.at[0, pl.ds((first + i) * per, per)]
            for turn in range(2):
                g = first + i
                remote(other, other, b_send.at[turn, g], b_recv.at[turn, g], b_peer).wait_recv()

                @pl.when(a == 1)
                def _():
                    remote(other, other, c_send.at[turn, g], c_recv.at[turn, g], sibling).wait_recv()
        term, d_gate, d_up = grads(
            product(first, small, 0, 0, me), product(first, small, 0, 1, me), product(first, small, 1, 2, me)
        )
        where = pl.ds(first, small)
        other_part[where] = results(d_gate, d_up, me, 1 - h, small)
        keep[0, where] = results(d_gate, d_up, me, h, small)
        n_rows = small * per * cap
        term_part[where] = jnp.broadcast_to(term, (n_rows, 128)).reshape(small, per * cap, 128)
        early(first, small, 0)

    lax.fori_loop(ahead, groups, forward_own, 0)
    for i in range(2, 8):
        local[i].wait()
    weight_landed(0)
    steps = groups // small

    def forward_mate(c, carry):
        @pl.when(c < steps)
        def _():
            for i in range(small):
                forward(mate, 1, c * small + i)

        @pl.when(c == steps)
        def _():
            weight_landed(1)
            for k in range(steps - 1):
                early(k * small, small, 1)

        @pl.when(c > 0)
        def _():
            own_quarter(c - 1)

        return carry

    lax.fori_loop(0, steps + 1, forward_mate, 0)
    early((steps - 1) * small, small, 1)
    weight_landed(2)

    def to_sibling(g):
        return (
            remote(keep.at[0, g], keep.at[1, g], k_send.at[0, g], k_recv.at[0, g], sibling),
            remote(term_half.at[0, g], term_half.at[1, g], k_send.at[1, g], k_recv.at[1, g], sibling),
        )

    def give_terms(g):
        @pl.when(a == 1)
        def _():
            to_sibling(g)[1].wait_recv()

        remote(term_half.at[0, g], term_in.at[g], t_send.at[g], t_recv.at[g], b_peer).wait_recv()
        term_ret[pl.ds(g * per, per)] = (term_half[a, g] + term_in[g])[:, None, :]

        def send(n):
            remote(
                term_ret.at[n], term_came.at[n], s_send.at[g], s_recv.at[g], origin(n, x)
            ).start()

        each(g * per, per, send)

    def give_back(g):
        @pl.when(a == 1)
        def _():
            to_sibling(g)[0].wait_recv()

        remote(psend.at[g], pin.at[g], p_send.at[g], p_recv.at[g], b_peer).wait_recv()
        total = (keep[a, g] + pin[g].astype(F32)).reshape(per, cap, half).astype(BF16)
        where = pl.ds(g * per, per)
        for q in range(2):
            ret[q, where] = total[:, :, q * part : (q + 1) * part]

        def send(side, n):
            q, plane = ((me, x), (mate, 2 * h + mate))[side]
            to = origin(n, plane)
            remote(ret.at[q, n], came.at[side, n], r_send.at[side, g], r_recv.at[side, g], to).start()

        for n in range(g * per, g * per + per):
            send(1, n)
            each(n, 1, functools.partial(send, 0))
        for early in (range(0, min(2, groups)) if g == 0 else range(g + 1, min(g + 2, groups))):
            give_terms(early)

    def mate_quarter(c, carry):
        first = c * small
        where = pl.ds(first, small)
        n_rows = small * per * cap
        term, d_gate, d_up = grads(
            pre[0, where].reshape(n_rows, -1),
            pre[1, where].reshape(n_rows, -1),
            product(first, small, 1, 2, mate),
        )
        term = term_part[where].reshape(n_rows, 128) + term
        lane = lax.broadcasted_iota(jnp.int32, (small * per, cap, 128), 2)
        at = lax.broadcasted_iota(jnp.int32, (small * per, cap, 128), 1)
        line = jnp.sum(jnp.where(lane == at, term.reshape(small * per, cap, 128), 0.0), axis=1)
        term_half[0, where] = line.reshape(small, per, 128)
        for i in range(small):
            g = first + i
            remote(term_half.at[0, g], term_in.at[g], t_send.at[g], t_recv.at[g], b_peer).start()

            @pl.when(a == 1)
            def _():
                to_sibling(first + i)[1].start()

        psend[where] = (other_part[where] + results(d_gate, d_up, mate, 1 - h, small)).astype(BF16)
        for i in range(small):
            g = first + i
            remote(psend.at[g], pin.at[g], p_send.at[g], p_recv.at[g], b_peer).start()
        keep[0, where] = keep[0, where] + results(d_gate, d_up, mate, h, small)
        for i in range(small):

            @pl.when(a == 1)
            def _():
                to_sibling(first + i)[0].start()

        return carry

    lax.fori_loop(0, steps, mate_quarter, 0)
    for copy in a_copies:
        copy.wait_send()

    def drain_rows(g, carry):
        for turn, q in enumerate((me, mate)):
            one_wait(
                g,
                sendb.at[q],
                lambda ref: remote(ref, ref, d_send.at[turn, g], d_recv.at[turn, g], b_peer).wait_send(),
            )
            ref = rows.at[landing(q), pl.ds(g * per, per)]
            remote(ref, ref, b_send.at[turn, g], b_recv.at[turn, g], b_peer).wait_send()

            @pl.when(a == 1)
            def _():
                remote(ref, ref, c_send.at[turn, g], c_recv.at[turn, g], sibling).wait_send()

        return carry

    lax.fori_loop(0, groups, drain_rows, 0)
    pl.semaphore_wait(ready, 1)
    for g in range(groups):
        give_back(g)

    came[0, 0] = ret[me, 0]
    term_came[0] = term_ret[0]

    def returned(g, ref, side, sends, recvs):
        act = lambda ref: remote(ref, ref, sends.at[side, g], recvs.at[side, g], b_peer).wait_recv()
        if side == 0:
            one_wait(g, ref.at[0], act)
        else:
            act(ref.at[1, pl.ds(g * per, per)])

    def landed(g, carry):
        for side in range(2):
            returned(g, came, side, r_send, r_recv)
        return carry

    mixed = 0.0
    cuts = (0, groups - groups // 4, groups) if groups > 4 else (0, groups)
    for first, last in zip(cuts, cuts[1:]):
        if last == groups:
            def terms_landed(g, carry):
                one_wait(
                    g, term_came, lambda ref: remote(ref, ref, s_send.at[g], s_recv.at[g], a_peer).wait_recv()
                )
                return carry

            lax.fori_loop(0, groups, terms_landed, 0)
            lane = lax.broadcasted_iota(jnp.int32, (peers, cap, 128), 2)
            at = lax.broadcasted_iota(jnp.int32, (peers, cap, 128), 1)
            line = term_came[...].reshape(peers, 128)
            seen = jnp.sum(jnp.where(lane == at, line[:, None, :], 0.0), axis=2, keepdims=True)
            by_expert = jnp.sum(hot[0].astype(F32).reshape(peers, cap, tokens) * seen, axis=1)
            for k in range(picks):
                same = ids[pl.ds(k, 1), :] == experts[0]
                part_t[pl.ds(k, 1), :] = jnp.sum(jnp.where(same, by_expert, 0.0), axis=0, keepdims=True)
            swap = remote(part_t, part_in, x_send.at[0], x_recv.at[0], a_peer)
            swap.start()
        lax.fori_loop(first, last, landed, 0)
        lanes = slice(first * per * cap, last * per * cap)
        for side in range(2):
            back_rows = came[side, first * per : last * per].astype(F32)
            back_rows = back_rows.reshape((last - first) * per * cap, part).astype(BF16)
            mixed += jnp.dot(mix_hi[side, :, lanes], back_rows, preferred_element_type=F32)
            mixed += jnp.dot(mix_lo[side, :, lanes], back_rows, preferred_element_type=F32)
    out[...] = mixed.astype(BF16)
    swap.wait()
    terms_out[...] = part_t[...] + part_in[...]

    def drain(g, carry):
        for side, q in enumerate((me, mate)):
            if side == 0:
                one_wait(
                    g,
                    ret.at[q],
                    lambda ref: remote(ref, ref, r_send.at[0, g], r_recv.at[0, g], b_peer).wait_send(),
                )
                one_wait(
                    g,
                    term_ret,
                    lambda ref: remote(ref, ref, s_send.at[g], s_recv.at[g], b_peer).wait_send(),
                )
            else:
                ref = ret.at[q, pl.ds(g * per, per)]
                remote(ref, ref, r_send.at[1, g], r_recv.at[1, g], b_peer).wait_send()
        remote(term_half.at[0, g], term_in.at[g], t_send.at[g], t_recv.at[g], b_peer).wait_send()

        @pl.when(a == 1)
        def _():
            for copy in to_sibling(g):
                copy.wait_send()

        remote(psend.at[g], pin.at[g], p_send.at[g], p_recv.at[g], b_peer).wait_send()
        return carry

    lax.fori_loop(0, groups, drain, 0)


def body(ny, nz, checkpoint, scales, out_grad, expert_ids, gates, w_gate, w_up, w_down):
    tokens, part = checkpoint.shape
    picks = expert_ids.shape[1]
    peers = ny * nz
    cap = tokens * picks // (2 * peers)
    hidden = w_gate.shape[1]
    half = 2 * part
    groups = max(2, peers // 8)
    group_rows = peers * cap // groups
    dma = pltpu.SemaphoreType.DMA
    vmem = pl.BlockSpec(memory_space=pltpu.VMEM)
    anyw = pl.BlockSpec(memory_space=pl.ANY)
    out, terms = pl.pallas_call(
        functools.partial(kernel, ny, nz),
        name="experts",
        out_shape=(
            jax.ShapeDtypeStruct((tokens, part), BF16),
            jax.ShapeDtypeStruct((picks, tokens), F32),
        ),
        in_specs=[vmem, vmem, vmem] + [anyw] * 5,
        out_specs=(vmem, vmem),
        scratch_shapes=[
            pltpu.VMEM((2, 2, tokens, part), BF16),
            pltpu.VMEM((2, groups, group_rows, tokens), BF16),
            pltpu.VMEM((2, tokens, peers * cap), BF16),
            pltpu.VMEM((2, tokens, peers * cap), BF16),
            pltpu.VMEM((2, peers, 2, cap, part), BF16),
            pltpu.VMEM((6, peers, 2, cap, part), BF16),
            pltpu.VMEM((3, 2, 2, hidden, half), BF16),
            pltpu.VMEM((groups, group_rows, half), BF16),
            pltpu.VMEM((groups, group_rows, half), BF16),
            pltpu.VMEM((2, groups, group_rows, half), F32),
            pltpu.VMEM((groups, group_rows, half), F32),
            pltpu.VMEM((groups, group_rows, 128), F32),
            pltpu.VMEM((2, groups, group_rows, hidden), F32),
            pltpu.VMEM((2, peers, cap, part), BF16),
            pltpu.VMEM((2, peers, cap, part), BF16),
            pltpu.VMEM((2, groups, peers // groups, 128), F32),
            pltpu.VMEM((groups, peers // groups, 128), F32),
            pltpu.VMEM((peers, 1, 128), F32),
            pltpu.VMEM((peers, 1, 128), F32),
            pltpu.VMEM((picks, tokens), F32),
            pltpu.VMEM((picks, tokens), F32),
            dma((8,)),
            dma((2,)),
            dma((2,)),
            dma((6,)),
            dma((6,)),
            dma((2, groups)),
            dma((2, groups)),
            dma((2, groups)),
            dma((2, groups)),
            dma((groups,)),
            dma((groups,)),
            dma((2, groups)),
            dma((2, groups)),
            dma((groups,)),
            dma((groups,)),
            dma((groups,)),
            dma((groups,)),
            dma((2, groups)),
            dma((2, groups)),
            dma((2, groups)),
            dma((2, groups)),
            dma((1,)),
            dma((1,)),
            pltpu.SemaphoreType.REGULAR,
        ],
        compiler_params=pltpu.CompilerParams(
            collective_id=0, has_side_effects=True, vmem_limit_bytes=60 * 1024 * 1024
        ),
    )(
        expert_ids.T,
        gates.T,
        scales[None, :],
        checkpoint,
        out_grad,
        w_gate[0],
        w_up[0],
        w_down[0],
    )
    return out, terms.T


def solution(mesh):
    n = mesh.shape["expert"]
    ny = 8 if n == 64 else n
    return jax.shard_map(
        functools.partial(body, ny, n // ny),
        mesh=mesh,
        in_specs=(
            P(("dp", "expert"), "tensor"),
            P(("dp", "expert")),
            P(("dp", "expert"), "tensor"),
            P(("dp", "expert"), None),
            P(("dp", "expert"), None),
            P(("dp", "expert"), "tensor", None),
            P(("dp", "expert"), "tensor", None),
            P(("dp", "expert"), "tensor", None),
        ),
        out_specs=(P(("dp", "expert"), "tensor"), P(("dp", "expert"), None)),
        check_vma=False,
    )
```

```python
import functools

import jax
import jax.numpy as jnp
from jax import lax
from jax.experimental import pallas as pl
from jax.experimental.pallas import tpu as pltpu
from jax.sharding import PartitionSpec as P

F32, BF16 = jnp.float32, jnp.bfloat16
NT = (((1,), (1,)), ((), ()))


def send_order(ny, nz):
    if (ny, nz) != (8, 8):
        return [(y, z) for y in range(ny) for z in range(nz)]

    def ring(u, v):
        images = []
        for y, z in ((u, v), (-u, -v), (v, -u), (-v, u)):
            if (y % ny, z % nz) not in images:
                images.append((y % ny, z % nz))
        return images

    return (
        (ring(0, 0) + ring(4, 4) + ring(0, 4) + ring(2, 2))
        + (ring(0, 1) + ring(3, 4))
        + (ring(0, 2) + ring(2, 4))
        + (ring(1, 1) + ring(3, 3))
        + (ring(0, 3) + ring(1, 4))
        + (ring(1, 2) + ring(2, 3))
        + (ring(1, -2) + ring(2, -3))
        + (ring(1, 3) + ring(1, -3))
    )


def kernel(
    ny,
    nz,
    ids,
    gates,
    scales,
    ck,
    og,
    wg,
    wu,
    wd,
    out,
    terms_out,
    raw,
    hot,
    mix_hi,
    mix_lo,
    sendb,
    rows,
    w,
    psend,
    pin,
    keep,
    other_part,
    term_part,
    pre,
    ret,
    came,
    term_half,
    term_in,
    term_ret,
    term_came,
    part_t,
    part_in,
    loc_sem,
    a_send,
    a_recv,
    w_send,
    w_recv,
    d_send,
    d_recv,
    b_send,
    b_recv,
    p_send,
    p_recv,
    r_send,
    r_recv,
    s_send,
    s_recv,
    t_send,
    t_recv,
    c_send,
    c_recv,
    k_send,
    k_recv,
    x_send,
    x_recv,
    ready,
):
    order = send_order(ny, nz)
    peers = ny * nz
    groups = keep.shape[1]
    per = peers // groups
    cap, part = sendb.shape[3:]
    half = 2 * part
    picks, tokens = ids.shape
    dp = lax.axis_index("dp")
    x = lax.axis_index("tensor")
    chip = lax.axis_index("expert")
    yy, zz = chip // nz, chip % nz
    h = x // 2
    a = (x + x // 2) % 2
    me = x % 2
    mate = 1 - me
    core = (dp + a) % 2
    a_peer = {"tensor": 2 * h + mate}
    b_peer = {"tensor": 3 - x, "dp": core}
    sibling = {"dp": 1 - dp}
    to_y = [((yy + d) % ny) * nz for d in range(ny)]
    to_z = [(zz + d) % nz for d in range(nz)]

    def target(n):
        y, z = order[n]
        return {"expert": to_y[y] + to_z[z]}

    def origin(n, plane):
        y, z = order[n]
        return {"tensor": plane, "expert": to_y[-y % ny] + to_z[-z % nz]}

    def landing(q):
        return (1 - a) * (2 * h + q) + a * (4 + q)

    def each(first, count, act):
        for n in range(max(first, 1), first + count):
            act(n)

    def remote(src, dst, send, recv, where):
        return pltpu.make_async_remote_copy(
            src_ref=src, dst_ref=dst, send_sem=send, recv_sem=recv, device_id=where
        )

    def one_wait(g, ref, wait):
        @pl.when(g > 0)
        def _():
            wait(ref.at[pl.ds(g * per, per)])

        if per > 1:

            @pl.when(g == 0)
            def _():
                wait(ref.at[pl.ds(1, per - 1)])

    weights = (wg, wu, wd)
    local = [
        pltpu.make_async_copy(ck, raw.at[me, 0], loc_sem.at[0]),
        pltpu.make_async_copy(og, raw.at[me, 1], loc_sem.at[1]),
    ]
    for m in range(3):
        for f in range(2):
            local.append(
                pltpu.make_async_copy(
                    weights[m].at[:, pl.ds(f * half, half)], w.at[m, me, f], loc_sem.at[2 + 2 * m + f]
                )
            )
    for copy in local:
        copy.start()

    barrier = pltpu.get_barrier_semaphore()
    for step in range(1, 4):
        pl.semaphore_signal(barrier, inc=1, device_id={"tensor": (x + step) % 4})
    pl.semaphore_signal(barrier, inc=1, device_id=sibling)
    pl.semaphore_signal(barrier, inc=1, device_id={"tensor": 3 - x, "dp": 1 - dp})
    for n in sorted(range(1, peers), key=lambda n: -sum(min(d, m - d) for d, m in zip(order[n], (ny, nz)))):
        pl.semaphore_signal(barrier, inc=1, device_id=target(n))

    r = lax.broadcasted_iota(jnp.int32, (peers, tokens), 0)
    expert = jnp.zeros((peers, tokens), jnp.int32)
    for n in range(peers):
        y, z = order[n]
        expert = jnp.where(r == n, core * peers + to_y[y] + to_z[z], expert)
    before = lax.broadcasted_iota(jnp.int32, (tokens, tokens), 0) < lax.broadcasted_iota(
        jnp.int32, (tokens, tokens), 1
    )
    before = before.astype(F32).astype(BF16)
    slot = lax.broadcasted_iota(jnp.int32, (peers, cap, tokens), 1).astype(F32)
    experts = (expert, expert + (1 - 2 * core) * peers)

    def choose(side):
        member = jnp.zeros((peers, tokens), F32)
        gate = jnp.zeros((peers, tokens), F32)
        for k in range(picks):
            same = ids[pl.ds(k, 1), :] == experts[side]
            member = jnp.where(same, 1.0, member)
            gate = jnp.where(same, gates[pl.ds(k, 1), :], gate)
        place = jnp.dot(member.astype(BF16), before, preferred_element_type=F32)
        place = jnp.where(member > 0.0, place, -1.0)
        pick = jnp.where(place[:, None, :] == slot, 1.0, 0.0)
        hot[side] = pick.reshape(groups, per * cap, tokens).astype(BF16)
        mix = (pick * gate[:, None, :]).reshape(peers * cap, tokens).T
        high = mix.astype(BF16)
        mix_hi[side] = high
        mix_lo[side] = (mix - high.astype(F32)).astype(BF16)

    choose(0)
    diagonal = lax.broadcasted_iota(jnp.int32, (tokens, tokens), 0) == lax.broadcasted_iota(
        jnp.int32, (tokens, tokens), 1
    )
    scale = jnp.sum(jnp.where(diagonal, scales[...], 0.0), axis=1, keepdims=True)

    def build(q):
        sources = ((raw[q, 0].astype(F32) * scale).astype(BF16), raw[q, 1])

        def group(g, carry):
            chosen = hot[0, g]
            for i in range(2):
                got = jnp.dot(chosen, sources[i], preferred_element_type=F32)
                sendb[q, pl.ds(g * per, per), i] = got.reshape(per, cap, part).astype(BF16)
            return carry

        lax.fori_loop(0, groups, group, 0)

        rows[landing(q), 0] = sendb[q, 0]

    def dispatch(q, turn):
        each(
            0,
            peers,
            lambda n: remote(
                sendb.at[q, n],
                rows.at[landing(q), n],
                d_send.at[turn, n // per],
                d_recv.at[turn, n // per],
                target(n),
            ).start(),
        )

    def forward(q, turn, g):
        one_wait(
            g,
            rows.at[landing(q)],
            lambda ref: remote(ref, ref, d_send.at[turn, g], d_recv.at[turn, g], b_peer).wait_recv(),
        )
        ref = rows.at[landing(q), pl.ds(g * per, per)]
        place = rows.at[2 * h + q, pl.ds(g * per, per)]
        remote(ref, place, b_send.at[turn, g], b_recv.at[turn, g], b_peer).start()

        @pl.when(a == 1)
        def _():
            remote(ref, place, c_send.at[turn, g], c_recv.at[turn, g], sibling).start()

    for i in range(2):
        local[i].wait()
    build(me)
    pl.semaphore_wait(barrier, peers + 4)
    pl.semaphore_signal(ready, inc=1, device_id=a_peer)

    a_copies = [
        remote(ck, raw.at[me, 0], a_send.at[0], a_recv.at[0], a_peer),
        remote(og, raw.at[me, 1], a_send.at[1], a_recv.at[1], a_peer),
    ]
    for m in range(3):
        for f in range(2):
            a_copies.append(
                remote(
                    weights[m].at[:, pl.ds(f * half, half)],
                    w.at[m, me, f],
                    w_send.at[2 * m + f],
                    w_recv.at[2 * m + f],
                    a_peer,
                )
            )
    for copy in a_copies:
        copy.start()
    dispatch(me, 0)
    choose(1)
    ahead = min(3, groups - 1)

    def forward_own(g, carry):
        forward(me, 0, g)
        return carry

    lax.fori_loop(0, ahead, forward_own, 0)
    for i in range(2):
        remote(ck, raw.at[mate, i], a_send.at[i], a_recv.at[i], a_peer).wait_recv()
    build(mate)
    dispatch(mate, 1)
    small = max(1, groups // 4)

    def product(first, count, i, m, q):
        total = 0.0
        for fq in range(4):
            lanes = slice((fq % 2) * part, (fq % 2 + 1) * part)
            value = rows[fq, pl.ds(first * per, count * per), i].astype(F32)
            value = value.reshape(count * per * cap, part).astype(BF16)
            total += lax.dot_general(
                value, w[m, q, fq // 2, :, lanes], NT, preferred_element_type=F32
            )
        return total

    def grads(gate_pre, up_pre, back):
        sigma = jax.nn.sigmoid(gate_pre)
        swish = gate_pre * sigma
        hidden = (swish * up_pre).astype(BF16)
        term = jnp.sum(hidden.astype(F32) * back, axis=1, keepdims=True)
        d_gate = (back * up_pre * sigma * (1.0 + gate_pre * (1.0 - sigma))).astype(BF16)
        d_up = (back * swish).astype(BF16)
        return term, d_gate, d_up

    def results(d_gate, d_up, q, f, count):
        result = jnp.dot(d_gate, w[0, q, f], preferred_element_type=F32)
        result = result + jnp.dot(d_up, w[1, q, f], preferred_element_type=F32)
        return result.reshape(count, per * cap, half)

    def weight_landed(m):
        for f in range(2):
            remote(
                w.at[m, mate, f], w.at[m, mate, f], w_send.at[2 * m + f], w_recv.at[2 * m + f], a_peer
            ).wait_recv()

    def early(first, count, m):
        value = product(first, count, 0, m, mate)
        pre[m, pl.ds(first, count)] = value.reshape(count, per * cap, value.shape[-1])

    def own_quarter(c):
        first = c * small
        for i in range(small):
            other = rows.at[0, pl.ds((first + i) * per, per)]
            for turn in range(2):
                g = first + i
                remote(other, other, b_send.at[turn, g], b_recv.at[turn, g], b_peer).wait_recv()

                @pl.when(a == 1)
                def _():
                    remote(other, other, c_send.at[turn, g], c_recv.at[turn, g], sibling).wait_recv()
        term, d_gate, d_up = grads(
            product(first, small, 0, 0, me), product(first, small, 0, 1, me), product(first, small, 1, 2, me)
        )
        where = pl.ds(first, small)
        other_part[where] = results(d_gate, d_up, me, 1 - h, small)
        keep[0, where] = results(d_gate, d_up, me, h, small)
        n_rows = small * per * cap
        term_part[where] = jnp.broadcast_to(term, (n_rows, 128)).reshape(small, per * cap, 128)
        early(first, small, 0)

    lax.fori_loop(ahead, groups, forward_own, 0)
    for i in range(2, 8):
        local[i].wait()
    weight_landed(0)
    steps = groups // small

    def forward_mate(c, carry):
        @pl.when(c < steps)
        def _():
            for i in range(small):
                forward(mate, 1, c * small + i)

        @pl.when(c == steps)
        def _():
            weight_landed(1)
            for k in range(steps - 1):
                early(k * small, small, 1)

        @pl.when(c > 0)
        def _():
            own_quarter(c - 1)

        return carry

    lax.fori_loop(0, steps + 1, forward_mate, 0)
    early((steps - 1) * small, small, 1)
    weight_landed(2)

    def to_sibling(g):
        return (
            remote(keep.at[0, g], keep.at[1, g], k_send.at[0, g], k_recv.at[0, g], sibling),
            remote(term_half.at[0, g], term_half.at[1, g], k_send.at[1, g], k_recv.at[1, g], sibling),
        )

    def give_terms(g):
        @pl.when(a == 1)
        def _():
            to_sibling(g)[1].wait_recv()

        remote(term_half.at[0, g], term_in.at[g], t_send.at[g], t_recv.at[g], b_peer).wait_recv()
        term_ret[pl.ds(g * per, per)] = (term_half[a, g] + term_in[g])[:, None, :]

        def send(n):
            remote(
                term_ret.at[n], term_came.at[n], s_send.at[g], s_recv.at[g], origin(n, x)
            ).start()

        each(g * per, per, send)

    def give_back(g):
        @pl.when(a == 1)
        def _():
            to_sibling(g)[0].wait_recv()

        remote(psend.at[g], pin.at[g], p_send.at[g], p_recv.at[g], b_peer).wait_recv()
        total = (keep[a, g] + pin[g].astype(F32)).reshape(per, cap, half).astype(BF16)
        where = pl.ds(g * per, per)
        for q in range(2):
            ret[q, where] = total[:, :, q * part : (q + 1) * part]

        def send(side, n):
            q, plane = ((me, x), (mate, 2 * h + mate))[side]
            to = origin(n, plane)
            remote(ret.at[q, n], came.at[side, n], r_send.at[side, g], r_recv.at[side, g], to).start()

        for n in range(g * per, g * per + per):
            send(1, n)
            each(n, 1, functools.partial(send, 0))
        for early in (range(0, min(2, groups)) if g == 0 else range(g + 1, min(g + 2, groups))):
            give_terms(early)

    def mate_quarter(c, carry):
        first = c * small
        where = pl.ds(first, small)
        n_rows = small * per * cap
        term, d_gate, d_up = grads(
            pre[0, where].reshape(n_rows, -1),
            pre[1, where].reshape(n_rows, -1),
            product(first, small, 1, 2, mate),
        )
        term = term_part[where].reshape(n_rows, 128) + term
        lane = lax.broadcasted_iota(jnp.int32, (small * per, cap, 128), 2)
        at = lax.broadcasted_iota(jnp.int32, (small * per, cap, 128), 1)
        line = jnp.sum(jnp.where(lane == at, term.reshape(small * per, cap, 128), 0.0), axis=1)
        term_half[0, where] = line.reshape(small, per, 128)
        for i in range(small):
            g = first + i
            remote(term_half.at[0, g], term_in.at[g], t_send.at[g], t_recv.at[g], b_peer).start()

            @pl.when(a == 1)
            def _():
                to_sibling(first + i)[1].start()

        psend[where] = (other_part[where] + results(d_gate, d_up, mate, 1 - h, small)).astype(BF16)
        for i in range(small):
            g = first + i
            remote(psend.at[g], pin.at[g], p_send.at[g], p_recv.at[g], b_peer).start()
        keep[0, where] = keep[0, where] + results(d_gate, d_up, mate, h, small)
        for i in range(small):

            @pl.when(a == 1)
            def _():
                to_sibling(first + i)[0].start()

        for early in range(min(1, steps - 2)):
            pl.when(c == early + 2)(functools.partial(give_back, early))
        return carry

    pl.semaphore_wait(ready, 1)
    lax.fori_loop(0, steps, mate_quarter, 0)
    for copy in a_copies:
        copy.wait_send()

    def drain_rows(g, carry):
        for turn, q in enumerate((me, mate)):
            one_wait(
                g,
                sendb.at[q],
                lambda ref: remote(ref, ref, d_send.at[turn, g], d_recv.at[turn, g], b_peer).wait_send(),
            )
            ref = rows.at[landing(q), pl.ds(g * per, per)]
            remote(ref, ref, b_send.at[turn, g], b_recv.at[turn, g], b_peer).wait_send()

            @pl.when(a == 1)
            def _():
                remote(ref, ref, c_send.at[turn, g], c_recv.at[turn, g], sibling).wait_send()

        return carry

    lax.fori_loop(0, groups, drain_rows, 0)
    for g in range(max(0, min(1, steps - 2)), groups):
        give_back(g)

    came[0, 0] = ret[me, 0]
    term_came[0] = term_ret[0]

    def returned(g, ref, side, sends, recvs):
        act = lambda ref: remote(ref, ref, sends.at[side, g], recvs.at[side, g], b_peer).wait_recv()
        if side == 0:
            one_wait(g, ref.at[0], act)
        else:
            act(ref.at[1, pl.ds(g * per, per)])

    def landed(g, carry):
        for side in range(2):
            returned(g, came, side, r_send, r_recv)
        return carry

    mixed = 0.0
    cuts = (0, groups - groups // 4, groups) if groups > 4 else (0, groups)
    for first, last in zip(cuts, cuts[1:]):
        if last == groups:
            def terms_landed(g, carry):
                one_wait(
                    g, term_came, lambda ref: remote(ref, ref, s_send.at[g], s_recv.at[g], a_peer).wait_recv()
                )
                return carry

            lax.fori_loop(0, groups, terms_landed, 0)
            lane = lax.broadcasted_iota(jnp.int32, (peers, cap, 128), 2)
            at = lax.broadcasted_iota(jnp.int32, (peers, cap, 128), 1)
            line = term_came[...].reshape(peers, 128)
            seen = jnp.sum(jnp.where(lane == at, line[:, None, :], 0.0), axis=2, keepdims=True)
            by_expert = jnp.sum(hot[0].astype(F32).reshape(peers, cap, tokens) * seen, axis=1)
            for k in range(picks):
                same = ids[pl.ds(k, 1), :] == experts[0]
                part_t[pl.ds(k, 1), :] = jnp.sum(jnp.where(same, by_expert, 0.0), axis=0, keepdims=True)
            swap = remote(part_t, part_in, x_send.at[0], x_recv.at[0], a_peer)
            swap.start()
        lax.fori_loop(first, last, landed, 0)
        lanes = slice(first * per * cap, last * per * cap)
        for side in range(2):
            back_rows = came[side, first * per : last * per].astype(F32)
            back_rows = back_rows.reshape((last - first) * per * cap, part).astype(BF16)
            mixed += jnp.dot(mix_hi[side, :, lanes], back_rows, preferred_element_type=F32)
            mixed += jnp.dot(mix_lo[side, :, lanes], back_rows, preferred_element_type=F32)
    out[...] = mixed.astype(BF16)
    swap.wait()
    terms_out[...] = part_t[...] + part_in[...]

    def drain(g, carry):
        for side, q in enumerate((me, mate)):
            if side == 0:
                one_wait(
                    g,
                    ret.at[q],
                    lambda ref: remote(ref, ref, r_send.at[0, g], r_recv.at[0, g], b_peer).wait_send(),
                )
                one_wait(
                    g,
                    term_ret,
                    lambda ref: remote(ref, ref, s_send.at[g], s_recv.at[g], b_peer).wait_send(),
                )
            else:
                ref = ret.at[q, pl.ds(g * per, per)]
                remote(ref, ref, r_send.at[1, g], r_recv.at[1, g], b_peer).wait_send()
        remote(term_half.at[0, g], term_in.at[g], t_send.at[g], t_recv.at[g], b_peer).wait_send()

        @pl.when(a == 1)
        def _():
            for copy in to_sibling(g):
                copy.wait_send()

        remote(psend.at[g], pin.at[g], p_send.at[g], p_recv.at[g], b_peer).wait_send()
        return carry

    lax.fori_loop(0, groups, drain, 0)


def body(ny, nz, checkpoint, scales, out_grad, expert_ids, gates, w_gate, w_up, w_down):
    tokens, part = checkpoint.shape
    picks = expert_ids.shape[1]
    peers = ny * nz
    cap = tokens * picks // (2 * peers)
    hidden = w_gate.shape[1]
    half = 2 * part
    groups = max(2, peers // 8)
    group_rows = peers * cap // groups
    dma = pltpu.SemaphoreType.DMA
    vmem = pl.BlockSpec(memory_space=pltpu.VMEM)
    anyw = pl.BlockSpec(memory_space=pl.ANY)
    out, terms = pl.pallas_call(
        functools.partial(kernel, ny, nz),
        name="experts",
        out_shape=(
            jax.ShapeDtypeStruct((tokens, part), BF16),
            jax.ShapeDtypeStruct((picks, tokens), F32),
        ),
        in_specs=[vmem, vmem, vmem] + [anyw] * 5,
        out_specs=(vmem, vmem),
        scratch_shapes=[
            pltpu.VMEM((2, 2, tokens, part), BF16),
            pltpu.VMEM((2, groups, group_rows, tokens), BF16),
            pltpu.VMEM((2, tokens, peers * cap), BF16),
            pltpu.VMEM((2, tokens, peers * cap), BF16),
            pltpu.VMEM((2, peers, 2, cap, part), BF16),
            pltpu.VMEM((6, peers, 2, cap, part), BF16),
            pltpu.VMEM((3, 2, 2, hidden, half), BF16),
            pltpu.VMEM((groups, group_rows, half), BF16),
            pltpu.VMEM((groups, group_rows, half), BF16),
            pltpu.VMEM((2, groups, group_rows, half), F32),
            pltpu.VMEM((groups, group_rows, half), F32),
            pltpu.VMEM((groups, group_rows, 128), F32),
            pltpu.VMEM((2, groups, group_rows, hidden), F32),
            pltpu.VMEM((2, peers, cap, part), BF16),
            pltpu.VMEM((2, peers, cap, part), BF16),
            pltpu.VMEM((2, groups, peers // groups, 128), F32),
            pltpu.VMEM((groups, peers // groups, 128), F32),
            pltpu.VMEM((peers, 1, 128), F32),
            pltpu.VMEM((peers, 1, 128), F32),
            pltpu.VMEM((picks, tokens), F32),
            pltpu.VMEM((picks, tokens), F32),
            dma((8,)),
            dma((2,)),
            dma((2,)),
            dma((6,)),
            dma((6,)),
            dma((2, groups)),
            dma((2, groups)),
            dma((2, groups)),
            dma((2, groups)),
            dma((groups,)),
            dma((groups,)),
            dma((2, groups)),
            dma((2, groups)),
            dma((groups,)),
            dma((groups,)),
            dma((groups,)),
            dma((groups,)),
            dma((2, groups)),
            dma((2, groups)),
            dma((2, groups)),
            dma((2, groups)),
            dma((1,)),
            dma((1,)),
            pltpu.SemaphoreType.REGULAR,
        ],
        compiler_params=pltpu.CompilerParams(
            collective_id=0, has_side_effects=True, vmem_limit_bytes=60 * 1024 * 1024
        ),
    )(
        expert_ids.T,
        gates.T,
        scales[None, :],
        checkpoint,
        out_grad,
        w_gate[0],
        w_up[0],
        w_down[0],
    )
    return out, terms.T


def solution(mesh):
    n = mesh.shape["expert"]
    ny = 8 if n == 64 else n
    return jax.shard_map(
        functools.partial(body, ny, n // ny),
        mesh=mesh,
        in_specs=(
            P(("dp", "expert"), "tensor"),
            P(("dp", "expert")),
            P(("dp", "expert"), "tensor"),
            P(("dp", "expert"), None),
            P(("dp", "expert"), None),
            P(("dp", "expert"), "tensor", None),
            P(("dp", "expert"), "tensor", None),
            P(("dp", "expert"), "tensor", None),
        ),
        out_specs=(P(("dp", "expert"), "tensor"), P(("dp", "expert"), None)),
        check_vma=False,
    )
```
